256 devices in a mesh: grp: 16 (over y, x), seq: 16 (over z, core).
Axes of the slice: x: 4, y: 4, z: 8, core: 2. Of those that a mesh axis runs over, the one named last changes fastest.
Arguments:
- audio: bfloat16 [16, 4096, 1280], P('grp', 'seq'), may hold values from -6 to 6, as said below
- block_ids: int32 [16, 4096], P('grp', 'seq'), may hold values from 0 to 80, never falling along the last dimension, each value on 1 to 100 neighbouring positions
- norm_gain: float32 [1280], replicated, may hold values from 0.1 to 1.9
- qkv_weight: bfloat16 [1280, 3840], P(None, 'grp'), may hold values from -8 to 8
- out_weight: bfloat16 [1280, 1280], P(None, 'grp'), may hold values from -0.15625 to 0.15625
- adapter_weight: bfloat16 [2560, 2048], P(None, 'grp'), may hold values from -0.125 to 0.125
- moe_gain: float32 [2048], replicated, may hold values from 0.1 to 1.9
- gate_weight: bfloat16 [16, 2048, 768], P('seq'), may hold values from -0.125 to 0.125
- up_weight: bfloat16 [16, 2048, 768], P('seq'), may hold values from -0.125 to 0.125
- down_weight: bfloat16 [16, 768, 2048], P('seq'), may hold values from -0.21875 to 0.21875
- routes: int32 [16, 2048, 4], P('grp', 'seq'), may hold values from 0 to 15, all different within a row; in each aligned block of 128 rows (0 to 127, 128 to 255, ..., all dimensions but the last counted through in order) at most 48 rows name the same one
- route_weights: float32 [16, 2048, 4], P('grp', 'seq'), may hold values from 0.05 to 1
Outputs:
- thinker_out: bfloat16 [16, 2048, 2048], P('grp', 'seq')
The draws below stay inside these ranges and needn't reach their ends.
Inputs may be any that keep to these rules, and one draw needn't show every extreme that they name: `audio`: in the hidden draw, frames come in nearly equal adjacent pairs. `block_ids`: block numbers never fall along a slab's frames; each block holds 1 to 100 frames, and some block exactly 100. `routes`: each token names 4 different experts; among the tokens of one device no expert is named by more than 48 of them, and in every draw some expert is named by exactly 48.
All inputs are finite; a program needn't handle non-finite values.
Results may differ from the reference program's by a relative error of at most 0.011.
Values may be sent and summed in bfloat16 or wider, within the bound.
No kernel may reach another device: no remote copies, remote signals or barrier semaphores. Data moves between devices by JAX's collectives and lax.ppermute only.
A program may use at most 128 MiB of HBM per device.

```python
import math
import jax
import jax.numpy as jnp
import numpy as np
from jax import lax

D = 1280
HEADS = 20
HEAD = 64
DM = 2048
FF = 768
TOK_DEV = 256
WIN = 100
TOPK = 4
EXPERTS = 16
CAP = 48
SLABS = 16
FRAMES = 4096
TOKENS = 2048
N_SEQ = 16


def draw_audio(key, part):
    base = jax.random.normal(key, (SLABS, FRAMES, D), jnp.float32)
    return jnp.clip(base, -6.0, 6.0).astype(jnp.bfloat16)


def draw_qkv_weight(key, part):
    weight = jax.random.normal(key, (D, 3 * D), jnp.float32) * D ** (-0.5)
    return jnp.clip(weight, -8.0, 8.0).astype(jnp.bfloat16)


def block_levels(stream_key, shape, cuts, low, top_value):
    def one(dim, parts):
        steps = jax.random.uniform(jax.random.fold_in(jax.random.fold_in(stream_key, 6), dim), (parts,), jnp.float32, low / len(cuts), top_value / len(cuts))
        return jnp.repeat(jnp.exp(steps), shape[dim] // parts).reshape((-1,) + (1,) * (len(shape) - dim - 1))

    loudness = one(*cuts[0])
    for cut in cuts[1:]:
        loudness = loudness * one(*cut)
    return loudness


def split_up(count, total, reach, lean):
    portions = [(1 << 20) // math.isqrt(grade ** lean) + 1 for grade in range(2, count + 1)]
    surplus, given = total - reach - (count - 1), [1] * (count - 1)
    while surplus > 0:
        movable = [i for i in range(count - 1) if given[i] < reach]
        pool, budget = sum([portions[i] for i in movable]), surplus
        for i in movable:
            extra = min(reach - given[i], max(1, budget * portions[i] // pool), surplus)
            given[i] = given[i] + extra
            surplus = surplus - extra
    return np.array([reach] + given)


def ragged_sizes(stream_key, amount, total, reach, lean):
    if amount == 2:
        one = jax.random.randint(stream_key, (), max(1, total - reach), min(reach, total - 1) + 1)
        return jnp.stack([one, total - one])
    lengths = jnp.asarray(split_up(amount, total, reach, lean), jnp.int32)
    twos = (amount - 1) // 2
    source_of, sink = lengths[1:1 + 2 * twos:2], lengths[2:2 + 2 * twos:2]
    room = jnp.minimum(source_of - 1, reach - sink)
    passed = jax.random.randint(jax.random.fold_in(stream_key, 1), (twos,), 0, 1 << 20) % (room + 1)
    lengths = lengths.at[1:1 + 2 * twos:2].set(source_of - passed).at[2:2 + 2 * twos:2].set(sink + passed)
    return lengths[jax.random.permutation(jax.random.fold_in(stream_key, 2), amount)]


def deal_out(key, own, number, rows, amount, top, limit, skew):
    ranking = jax.random.permutation(key, amount)
    heavy_load, common = load_shares(amount, rows * top, limit, skew, True), load_shares(amount, rows * top, limit, skew, False)
    places = jnp.arange(amount)

    def named(lengths, rotation):
        used = int((lengths > 0).sum())
        fixed = max(1, used // 4)
        moved = fixed + (places - fixed + rotation * (used - fixed)) % max(1, amount - fixed)
        return jnp.zeros((amount,), jnp.int32).at[ranking[jnp.where(places < fixed, places, moved)]].set(jnp.asarray(lengths, jnp.int32))

    lengths = jnp.where(number % 4 == 0, named(heavy_load, number // 4), named(common, number - number // 4 - 1))
    mixed = jax.random.permutation(jax.random.fold_in(own, 3), amount)
    source_of, taker = mixed[0:amount // 2 * 2:2], mixed[1:amount // 2 * 2:2]
    room = jnp.minimum(lengths[source_of] - 1, limit - lengths[taker]) // 2
    room = jnp.where((source_of == ranking[0]) | (taker == ranking[0]) | (lengths[taker] == 0), 0, jnp.maximum(room, 0))
    moved = jax.random.randint(jax.random.fold_in(own, 4), (amount // 2,), 0, 1 << 20) % (room + 1)
    lengths = lengths.at[source_of].add(-moved).at[taker].add(moved)
    members = jnp.searchsorted(jnp.cumsum(lengths), jnp.arange(rows * top), side="right").astype(jnp.int32)
    grid = members.reshape(top, rows).T
    grid = grid[jax.random.permutation(jax.random.fold_in(own, 1), rows)]
    rotation = jax.random.randint(jax.random.fold_in(own, 2), (rows, 1), 0, top)
    return jnp.take_along_axis(grid, (jnp.arange(top)[None, :] + rotation) % top, axis=1)


def load_shares(amount, total, limit, lean, full):
    portions = [(1 << 20) // math.isqrt(rank ** lean) + 1 for rank in range(1, amount + 1)]
    largest = limit if full else min(limit, max(-(-total // amount), total * portions[0] // sum(portions)))
    least = 1 if total - largest >= amount - 1 else 0
    holding, surplus = [largest] + [least] * (amount - 1), total - largest - least * (amount - 1)
    while surplus > 0:
        movable = [i for i in range(1, amount) if holding[i] < largest] or [i for i in range(1, amount) if holding[i] < limit]
        pool, remaining = sum([portions[i] for i in movable]), surplus
        for i in movable:
            more = min(limit - holding[i], max(1, remaining * portions[i] // pool), surplus)
            holding[i] = holding[i] + more
            surplus = surplus - more
    return np.array(holding)


def bell_draw(own_key, extent, width, bound, cuts=(), kind=jnp.bfloat16):
    level = block_levels(own_key, extent, cuts, -0.22, 0.18) if cuts else 1.0
    drawn = jax.random.normal(own_key, extent, jnp.float32) * width * level
    return jnp.minimum(jnp.maximum(drawn, -bound), bound).astype(kind)


def setup_inputs(seed: int = 0) -> dict:
    seeds = jax.random.split(jax.random.key(seed), 13)
    audio = draw_audio(jax.random.fold_in(seeds[12], 71), 0)
    block_ids = jax.vmap(lambda own: jnp.searchsorted(jnp.cumsum(ragged_sizes(own, 2 * FRAMES // WIN, FRAMES, WIN, 1)), jnp.arange(FRAMES), side="right"))(jax.random.split(seeds[1], SLABS)).reshape((SLABS, FRAMES)).astype(jnp.int32)
    norm_gain = jnp.clip(1.0 + 0.18 * jax.random.normal(seeds[2], (D,), jnp.float32), 0.1, 1.9)
    qkv_weight = draw_qkv_weight(jax.random.fold_in(seeds[12], 71), 0)
    out_weight = bell_draw(seeds[4], (D, D), D ** -0.5, 0.15625, ((1, 16),))
    adapter_weight = bell_draw(seeds[5], (2 * D, DM), (2 * D) ** -0.5, 0.125, ((1, 16),))
    moe_gain = jnp.clip(1.0 + 0.18 * jax.random.normal(seeds[6], (DM,), jnp.float32), 0.1, 1.9)
    gate_weight = bell_draw(seeds[7], (EXPERTS, DM, FF), DM ** -0.5, 0.125, ((0, 16),))
    up_weight = bell_draw(seeds[8], (EXPERTS, DM, FF), DM ** -0.5, 0.125, ((0, 16),))
    down_weight = bell_draw(seeds[9], (EXPERTS, FF, DM), FF ** -0.5, 0.21875, ((0, 16),))
    routes_keys = jax.random.split(jax.random.fold_in(seeds[10], 1), SLABS * TOKENS // (TOK_DEV // 2))
    routes_turns = jax.random.permutation(jax.random.fold_in(seeds[10], 3), SLABS * TOKENS // (TOK_DEV // 2))
    routes = jax.vmap(lambda own, number: deal_out(jax.random.fold_in(seeds[10], 2), own, number, TOK_DEV // 2, EXPERTS, TOPK, CAP, 2))(routes_keys, routes_turns).reshape((SLABS, TOKENS, TOPK))
    route_weights = jnp.clip(jnp.exp(math.log(1.0) - 2.9957323 * jax.random.uniform(seeds[11], (SLABS, TOKENS, TOPK), jnp.float32) ** block_levels(seeds[11], (SLABS, TOKENS, TOPK), ((0, 16), (1, 16)), -0.2, 0.2)), 0.05, 1.0)
    return dict(audio=audio, block_ids=block_ids, norm_gain=norm_gain, qkv_weight=qkv_weight, out_weight=out_weight, adapter_weight=adapter_weight, moe_gain=moe_gain, gate_weight=gate_weight, up_weight=up_weight, down_weight=down_weight, routes=routes, route_weights=route_weights)


LN_EPSILON = 1e-05
RMS_EPSILON = 1e-06
MASKED = -1e+30

def layer_norm(signal, gain):
    widened = signal.astype(jnp.float32)
    average = lax.optimization_barrier(jnp.mean(widened, axis=-1, keepdims=True))
    centred = widened - average
    variance = lax.optimization_barrier(jnp.mean(centred * centred, axis=-1, keepdims=True))
    return centred * lax.rsqrt(variance + LN_EPSILON) * gain

def rms_norm(signal, gain):
    widened = signal.astype(jnp.float32)
    squares = lax.optimization_barrier(jnp.mean(widened * widened, axis=-1, keepdims=True))
    return widened * lax.rsqrt(squares + RMS_EPSILON) * gain

def slab_attention(slab_qkv, slab_ids):
    margin = WIN - 1
    query_all = slab_qkv[:, :D]
    padded = jnp.pad(slab_qkv[:, D:], ((margin, margin), (0, 0)))
    padded_ids = jnp.pad(slab_ids, (margin, margin), constant_values=-1)

    def one_block(block_number):
        first_row = (block_number * TOK_DEV).astype(jnp.int32)
        query_rows = lax.dynamic_slice_in_dim(query_all, first_row, TOK_DEV, 0).reshape(TOK_DEV, HEADS, HEAD)
        query_ids = lax.dynamic_slice_in_dim(slab_ids, first_row, TOK_DEV, 0)
        window = lax.dynamic_slice_in_dim(padded, first_row, TOK_DEV + 2 * margin, 0)
        window_ids = lax.dynamic_slice_in_dim(padded_ids, first_row, TOK_DEV + 2 * margin, 0)
        key_rows = window[:, :D].reshape(-1, HEADS, HEAD).astype(jnp.float32)
        value_rows = window[:, D:].reshape(-1, HEADS, HEAD).astype(jnp.float32)
        scores = jnp.einsum('qhd,khd->hqk', query_rows.astype(jnp.float32), key_rows) * HEAD ** (-0.5)
        allowed = query_ids[:, None] == window_ids[None, :]
        scores = jnp.where(allowed[None], scores, MASKED)
        highest = lax.optimization_barrier(jnp.max(scores, axis=-1, keepdims=True))
        exponent = jnp.exp(scores - highest)
        probability = (exponent / lax.optimization_barrier(jnp.sum(exponent, axis=-1, keepdims=True))).astype(jnp.bfloat16)
        attended = jnp.einsum('hqk,khd->qhd', probability.astype(jnp.float32), value_rows)
        return attended.astype(jnp.bfloat16).reshape(TOK_DEV, D)
    blocks = lax.map(one_block, jnp.arange(N_SEQ, dtype=jnp.int32))
    return blocks.reshape(FRAMES, D)

def reference(audio, block_ids, norm_gain, qkv_weight, out_weight, adapter_weight, moe_gain, gate_weight, up_weight, down_weight, routes, route_weights):
    flat_audio = audio.reshape(SLABS * FRAMES, D)
    normed = layer_norm(flat_audio, norm_gain).astype(jnp.bfloat16)
    qkv_all = jnp.dot(normed, qkv_weight, preferred_element_type=jnp.float32).astype(jnp.bfloat16)
    qkv_all = qkv_all.reshape(SLABS, FRAMES, 3 * D)
    attended = lax.map(lambda pair: slab_attention(pair[0], pair[1]), (qkv_all, block_ids))
    attended = attended.reshape(SLABS * FRAMES, D)
    projected = jnp.dot(attended, out_weight, preferred_element_type=jnp.float32)
    encoded = (flat_audio.astype(jnp.float32) + projected).astype(jnp.bfloat16)
    pooled = encoded.reshape(SLABS * TOKENS, 2 * D)
    thinker_in = jnp.dot(pooled, adapter_weight, preferred_element_type=jnp.float32).astype(jnp.bfloat16)
    expert_in = rms_norm(thinker_in, moe_gain).astype(jnp.bfloat16)
    block_count = SLABS * N_SEQ
    per_block = TOKENS // N_SEQ
    flat_routes = routes.reshape(block_count, per_block * TOPK).astype(jnp.int32)
    expert_ids = jnp.arange(EXPERTS, dtype=jnp.int32)
    membership = (flat_routes[:, :, None] == expert_ids[None, None, :]).astype(jnp.int32)
    positions = lax.optimization_barrier(jnp.sum((jnp.cumsum(membership, axis=1) - 1) * membership, axis=2))
    slot_index = flat_routes * CAP + positions
    block_index = jnp.arange(block_count, dtype=jnp.int32)[:, None]
    token_index = block_index * per_block + jnp.arange(per_block * TOPK, dtype=jnp.int32)[None, :] // TOPK
    shares = route_weights / lax.optimization_barrier(jnp.sum(route_weights, axis=-1, keepdims=True))
    shares = shares.reshape(block_count, per_block * TOPK)
    token_table = jnp.zeros((block_count, EXPERTS * CAP), jnp.int32).at[block_index, slot_index].set(token_index)
    share_table = jnp.zeros((block_count, EXPERTS * CAP), jnp.float32).at[block_index, slot_index].set(shares)
    token_table = token_table.reshape(block_count, EXPERTS, CAP).transpose(1, 0, 2).reshape(EXPERTS, block_count * CAP)
    share_table = share_table.reshape(block_count, EXPERTS, CAP).transpose(1, 0, 2).reshape(EXPERTS, block_count * CAP)

    def one_expert(running, inputs):
        token_rows, row_shares, gate_matrix, up_matrix, down_matrix = inputs
        routed_rows = expert_in[token_rows]
        gate_act = jnp.dot(routed_rows, gate_matrix, preferred_element_type=jnp.float32)
        up_act = jnp.dot(routed_rows, up_matrix, preferred_element_type=jnp.float32)
        hidden = (jax.nn.silu(gate_act) * up_act).astype(jnp.bfloat16)
        produced = jnp.dot(hidden, down_matrix, preferred_element_type=jnp.float32).astype(jnp.bfloat16)
        running = running.at[token_rows].add(row_shares[:, None] * produced.astype(jnp.float32))
        return (running, None)
    start_value = thinker_in.astype(jnp.float32)
    running, unused = lax.scan(one_expert, start_value, (token_table, share_table, gate_weight, up_weight, down_weight))
    return running.astype(jnp.bfloat16).reshape(SLABS, TOKENS, DM)
```

```python
import functools

import jax
import jax.numpy as jnp
from jax import lax
from jax.experimental import pallas as pl
from jax.experimental.pallas import tpu as pltpu
from jax.sharding import Mesh
from jax.sharding import PartitionSpec as P

HEADS = 20
HEAD = 64
D = 1280
DM = 2048
FF = 768
CAP = 48
GRP = ("y", "x")
SEQ = ("z", "core")
ALL = ("y", "x", "z", "core")
NY, NX, NZ = 4, 4, 8
LN_EPSILON = 1e-05
RMS_EPSILON = 1e-06
MASKED = -1e30
BF = jnp.bfloat16
F32 = jnp.float32

REL = (0, -1, 1, 2)
ZREL = (0, -1, 1, -2, 2, -3, 3, 4)
QKV_SPLIT = (128, 112)
OA_SPLIT = (832, 848)
HALF = DM // 2


def flat(y, x, z, c):
    return (((y % NY) * NX + x % NX) * NZ + z % NZ) * 2 + c


def grp_perm(phase, sign):
    pairs = []
    for y in range(NY):
        for x in range(NX):
            for z in range(NZ):
                for c in range(2):
                    along_x = (c == 0) == (phase == 0)
                    dst = flat(y, x + sign, z, c) if along_x else flat(y + sign, x, z, c)
                    pairs.append((flat(y, x, z, c), dst))
    return pairs


def swap_cores(value):
    return lax.ppermute(value, "core", [(0, 1), (1, 0)])


def shift_z(value, sign):
    return lax.ppermute(value, "z", [(i, (i + sign) % NZ) for i in range(NZ)])


def ring4(parts, phase):
    up, down = grp_perm(phase, 1), grp_perm(phase, -1)
    move = functools.partial(lax.ppermute, axis_name=ALL)
    a0, b1 = move(parts[0], perm=up), move(parts[1], perm=down)
    a1, b0 = move(parts[1], perm=up), move(parts[0], perm=down)
    o0, o1 = move(a0, perm=up), move(b1, perm=down)
    return (tuple(parts), (a0, a1), (b0, b1), (o0, o1))


def gather_weights(parts):
    first = ring4(parts, 0)
    blocks = [jnp.stack([first[i][j] for i in range(4)]) for j in range(2)]
    own = ring4(blocks, 1)
    other = tuple(tuple(swap_cores(v) for v in pair) for pair in own)
    return own, other


def layer_norm(signal, gain):
    widened = signal.astype(F32)
    average = jnp.mean(widened, axis=-1, keepdims=True)
    centred = widened - average
    variance = jnp.mean(centred * centred, axis=-1, keepdims=True)
    return centred * lax.rsqrt(variance + LN_EPSILON) * gain


def nn(a, b):
    return lax.dot_general(a, b, (((1,), (0,)), ((), ())), preferred_element_type=F32)


def attention_kernel(tab, nt, idk, idq, *refs):
    pieces, (out, w, qkv, bias, sems) = refs[:16], refs[16:]
    core = tab[0]
    copies = []
    for side in range(2):
        for p in range(4):
            for j in range(2):
                for i in range(4):
                    g = tab[2 + side * 16 + p * 4 + i]
                    row = pl.multiple_of(g * 240 + j * 128, 16)
                    copy = pltpu.make_async_copy(
                        pieces[side * 8 + p * 2 + j].at[i],
                        w.at[side, pl.ds(row, QKV_SPLIT[j]), :],
                        sems.at[len(copies)],
                    )
                    copy.start()
                    copies.append(copy)
    bias[...] = jnp.where(idk[...] == idq[...], 0.0, MASKED)
    for copy in copies:
        copy.wait()
    own = pl.ds(pl.multiple_of(core * 640, 128), 640)
    oth = pl.ds(pl.multiple_of(640 - core * 640, 128), 640)

    def query_rows(m, carry):
        rows = pl.ds(pl.multiple_of(m * 320, 64), 320)
        acc = nn(w[0, rows, :], nt[own, 0:256]) + nn(w[1, rows, :], nt[oth, 0:256])
        qkv[rows, 0:256] = acc.astype(BF) * BF(HEAD**-0.5)
        return carry

    def pair_rows(m, carry):
        rows = pl.ds(pl.multiple_of(m * 320, 64), 320)
        acc = nn(w[0, rows, :], nt[own, :]) + nn(w[1, rows, :], nt[oth, :])
        qkv[rows, :] = acc.astype(BF)
        return carry

    lax.fori_loop(0, 4, query_rows, 0)
    lax.fori_loop(4, 12, pair_rows, 0)

    def one_head(h):
        base = h * HEAD
        q = qkv[pl.ds(pl.multiple_of(base, 64), HEAD), 0:256]
        k = qkv[pl.ds(pl.multiple_of(D + base, 64), HEAD), :]
        v = qkv[pl.ds(pl.multiple_of(2 * D + base, 64), HEAD), :]
        s = nn(k.T, q) + bias[...]
        top = jnp.max(s, axis=0, keepdims=True)
        e = jnp.exp(s - top)
        total = jnp.sum(e, axis=0, keepdims=True)
        o = nn(v, e.astype(BF)) / total
        out[pl.ds(pl.multiple_of(base, 64), HEAD), :] = o.astype(BF)

    def heads(n, carry):
        one_head(2 * n)
        one_head(2 * n + 1)
        return carry

    lax.fori_loop(0, HEADS // 2, heads, 0)


def tail_kernel(tab, att, audio_t, gain, *refs):
    pieces = refs[:16]
    thinker, x0, x1, w, wo, enc_t, acc, sems = refs[16:]
    core = tab[0]
    copies = []
    for side in range(2):
        for p in range(4):
            for j in range(2):
                for i in range(4):
                    copy = pltpu.make_async_copy(
                        pieces[side * 8 + p * 2 + j].at[i],
                        w.at[side, p * 4 + i, pl.ds(OA_SPLIT[0] * j, OA_SPLIT[j]), :],
                        sems.at[len(copies)],
                    )
                    copy.start()
                    copies.append(copy)
    for copy in copies:
        copy.wait()
    for side in range(2):
        for s in range(16):
            row = pl.multiple_of(tab[2 + side * 16 + s] * 80, 16)
            for k in range(5):
                wo[side, pl.ds(row, 80), k * 128 : (k + 1) * 128] = w[side, s, k * 80 : (k + 1) * 80, :]
    own = pl.ds(pl.multiple_of(core * 640, 128), 640)
    oth = pl.ds(pl.multiple_of(640 - core * 640, 128), 640)

    def project(m, carry):
        rows = pl.ds(pl.multiple_of(m * 320, 64), 320)
        projected = nn(wo[0, rows, :], att[own, :]) + nn(wo[1, rows, :], att[oth, :])
        enc_t[rows, :] = (audio_t[rows, :].astype(F32) + projected).astype(BF)
        return carry

    lax.fori_loop(0, 4, project, 0)
    even = enc_t[:, 0:128].T
    odd = enc_t[:, 128:256].T
    first = core == 0
    mine = jnp.where(first, even, odd)
    rest = jnp.where(first, odd, even)
    for p in range(4):
        for i in range(4):
            s, t = p * 4 + i, i * 4 + p
            g = tab[2 + s]
            block = nn(mine, w[0, s, 400:1680, :]) + nn(rest, w[1, t, 400:1680, :])
            acc[:, pl.ds(pl.multiple_of(g * 128, 128), 128)] = block
    rounded = acc[...].astype(BF)
    thinker[...] = rounded
    widened = rounded.astype(F32)
    squares = jnp.mean(widened * widened, axis=1, keepdims=True)
    normed = (widened * lax.rsqrt(squares + RMS_EPSILON) * gain[...]).astype(BF)
    x0[...] = normed[:, :HALF]
    x1[...] = normed[:, HALF:]


def expert_kernel(tab, meta_row, meta_col, *refs):
    xs, weights = refs[:16], refs[16:22]
    outs = refs[22:38]
    wg, wu, wd, xg, hid, yg, dsel, share, sems = refs[38:]
    core, z = tab[0], tab[1]
    copies = []
    for n, (src, dst) in enumerate(
        zip(weights, (wg.at[0], wu.at[0], wd.at[0], wg.at[1], wu.at[1], wd.at[1]))
    ):
        copy = pltpu.make_async_copy(src, dst, sems.at[n])
        copy.start()
        copies.append(copy)
    e0 = (2 * z + core).astype(F32)
    e1 = (2 * z + 1 - core).astype(F32)
    lane = lax.broadcasted_iota(jnp.int32, (128, 128), 1)
    sub = lax.broadcasted_iota(jnp.int32, (128, 128), 0)
    lane_expert = jnp.where(lane < CAP, e0, e1)
    sub_expert = jnp.where(sub < CAP, e0, e1)
    lane_slot = jnp.where(lane < CAP, lane, lane - CAP).astype(F32)
    earlier = jnp.where(lane < sub, 1.0, 0.0).astype(BF)
    for r in range(8):
        source = lax.rem(z + (ZREL[r] + 8), 8)
        mc = meta_col[source]
        mr = meta_row[source]
        chosen = jnp.zeros((128, 128), F32)
        weight = jnp.zeros((128, 128), F32)
        for k in range(4):
            chosen = jnp.where(mc[:, k : k + 1] == lane_expert, 1.0, chosen)
            weight = jnp.where(mr[k : k + 1, :] == sub_expert, mr[4 + k : 5 + k, :], weight)
        place = nn(earlier, chosen.astype(BF))
        scatter = jnp.where((place == lane_slot) & (lane < 2 * CAP), chosen, 0.0)
        select = scatter.T
        dsel[r] = scatter.astype(BF)
        share[r] = jnp.broadcast_to(jnp.sum(select * weight, axis=1, keepdims=True), (128, 128))
        pick = select[: 2 * CAP].astype(BF)
        for j in range(2):
            rows = nn(pick, xs[2 * r + j][...]).astype(BF)
            xg[0, r * CAP : (r + 1) * CAP, j * HALF : (j + 1) * HALF] = rows[:CAP]
            xg[1, r * CAP : (r + 1) * CAP, j * HALF : (j + 1) * HALF] = rows[CAP:]
        yg[r, 2 * CAP :, :] = jnp.zeros((128 - 2 * CAP, DM), BF)
    for e in range(2):
        copies[3 * e].wait()
        copies[3 * e + 1].wait()

        def up(n, carry):
            cols = pl.ds(pl.multiple_of(n * 256, 256), 256)
            gate_act = nn(xg[e], wg[e, :, cols])
            up_act = nn(xg[e], wu[e, :, cols])
            hid[:, cols] = (gate_act / (1.0 + jnp.exp(-gate_act)) * up_act).astype(BF)
            return carry

        lax.fori_loop(0, FF // 256, up, 0)
        copies[3 * e + 2].wait()

        def down(n, carry):
            cols = pl.ds(pl.multiple_of(n * 512, 512), 512)
            made = nn(hid[...], wd[e, :, cols])
            for r in range(8):
                scale = share[r, e * CAP : (e + 1) * CAP, 0:1]
                yg[r, e * CAP : (e + 1) * CAP, cols] = (
                    made[r * CAP : (r + 1) * CAP] * scale
                ).astype(BF)
            return carry

        lax.fori_loop(0, DM // 512, down, 0)
    for r in range(8):
        for j in range(2):
            outs[2 * r + j][...] = nn(dsel[r], yg[r, :, j * HALF : (j + 1) * HALF]).astype(BF)


VMEM = pl.BlockSpec(memory_space=pltpu.VMEM)
SMEM = pl.BlockSpec(memory_space=pltpu.SMEM)
ANY = pl.BlockSpec(memory_space=pl.ANY)


def shape(*dims, dtype=BF):
    return jax.ShapeDtypeStruct(dims, dtype)


def body(
    audio,
    block_ids,
    norm_gain,
    qkv_weight,
    out_weight,
    adapter_weight,
    moe_gain,
    gate_weight,
    up_weight,
    down_weight,
    routes,
    route_weights,
):
    y, x = lax.axis_index("y"), lax.axis_index("x")
    z, core = lax.axis_index("z"), lax.axis_index("core")

    qkv_t = lax.dynamic_slice_in_dim(qkv_weight.T, core * 640, 640, 1)
    qkv_own, qkv_other = gather_weights([qkv_t[:128], qkv_t[128:]])
    out_t = lax.dynamic_slice_in_dim(out_weight.T, core * 640, 640, 1)
    out_t = out_t.reshape(80, 5, 128).transpose(1, 0, 2).reshape(400, 128)
    ada = lax.dynamic_slice_in_dim(adapter_weight, core * D, D, 0)
    oa_own, oa_other = gather_weights([jnp.concatenate([out_t, ada[:432]]), ada[432:]])

    expert_other = [swap_cores(v[0]) for v in (gate_weight, up_weight, down_weight)]

    signal = audio[0]
    count = NZ * 2
    ahead = [(i, i + 1) for i in range(count - 1)]
    back = [(i + 1, i) for i in range(count - 1)]
    left = lax.ppermute(signal[128:], SEQ, ahead)
    right = lax.ppermute(signal[:128], SEQ, back)
    paired = signal.reshape(128, 2, D)
    extended = jnp.concatenate([paired[:, 0], paired[:, 1], left, right])
    normed_t = layer_norm(extended, norm_gain).astype(BF).T
    audio_t = extended[:256].T
    ids = block_ids[0] + 1
    ids_left = lax.ppermute(ids[128:], SEQ, ahead)
    ids_right = lax.ppermute(ids[:128], SEQ, back)
    ids_paired = ids.reshape(128, 2)
    ids_all = jnp.concatenate([ids_paired[:, 0], ids_paired[:, 1], ids_left, ids_right])
    ids_all = ids_all.astype(F32)

    weights_here = route_weights[0]
    shares = weights_here / jnp.sum(weights_here, axis=1, keepdims=True)
    meta = jnp.concatenate([routes[0].astype(F32).T, shares.T])
    meta_row = lax.all_to_all(
        jnp.broadcast_to(meta[None], (NZ, 8, 128)), "z", split_axis=0, concat_axis=0, tiled=True
    )
    meta_col = meta_row.transpose(0, 2, 1)

    rel = jnp.array(REL, jnp.int32)
    at_y, at_x = (y + rel) % NY, (x + rel) % NX
    table0 = at_y[:, None] * NX + at_x[None, :]
    table1 = at_y[None, :] * NX + at_x[:, None]
    own_table = jnp.where(core == 0, table0, table1).reshape(-1)
    other_table = jnp.where(core == 0, table1, table0).reshape(-1)
    tab = jnp.concatenate([jnp.stack([core, z]), own_table, other_table]).astype(jnp.int32)

    attended_t = pl.pallas_call(
        attention_kernel,
        out_shape=shape(D, 256),
        in_specs=[SMEM, VMEM, VMEM, VMEM] + [ANY] * 16,
        out_specs=VMEM,
        scratch_shapes=[
            pltpu.VMEM((2, 3 * D, 640), BF),
            pltpu.VMEM((3 * D, 512), BF),
            pltpu.VMEM((512, 256), F32),
            pltpu.SemaphoreType.DMA((64,)),
        ],
        cost_estimate=pl.CostEstimate(flops=7 * 10**9, bytes_accessed=12 * 10**6, transcendentals=3 * 10**6),
        name="attention",
    )(
        tab,
        normed_t,
        ids_all[:, None],
        ids_all[None, :256],
        *[v for pair in qkv_own for v in pair],
        *[v for pair in qkv_other for v in pair],
    )

    thinker_in, x0, x1 = pl.pallas_call(
        tail_kernel,
        out_shape=[shape(128, DM), shape(128, HALF), shape(128, HALF)],
        in_specs=[SMEM, VMEM, VMEM, VMEM] + [ANY] * 16,
        out_specs=[VMEM] * 3,
        scratch_shapes=[
            pltpu.VMEM((2, 16, 1680, 128), BF),
            pltpu.VMEM((2, D, 640), BF),
            pltpu.VMEM((D, 256), BF),
            pltpu.VMEM((128, DM), F32),
            pltpu.SemaphoreType.DMA((64,)),
        ],
        cost_estimate=pl.CostEstimate(flops=3 * 10**9, bytes_accessed=16 * 10**6, transcendentals=0),
        name="tail",
    )(
        tab,
        attended_t,
        audio_t,
        moe_gain[None],
        *[v for pair in oa_own for v in pair],
        *[v for pair in oa_other for v in pair],
    )

    up0, up1, down0, down1 = [x0], [x1], [x0], [x1]
    for step in range(4):
        up0.append(shift_z(up0[-1], 1))
        down1.append(shift_z(down1[-1], -1))
        if step < 3:
            up1.append(shift_z(up1[-1], 1))
            down0.append(shift_z(down0[-1], -1))
    tokens = []
    for off in ZREL:
        if off == 4:
            tokens += [up0[4], down1[4]]
        elif off <= 0:
            tokens += [up0[-off], up1[-off]]
        else:
            tokens += [down0[off], down1[off]]

    partial = pl.pallas_call(
        expert_kernel,
        out_shape=[shape(128, HALF)] * 16,
        in_specs=[SMEM, VMEM, VMEM] + [VMEM] * 16 + [ANY] * 6,
        out_specs=[VMEM] * 16,
        scratch_shapes=[
            pltpu.VMEM((2, DM, FF), BF),
            pltpu.VMEM((2, DM, FF), BF),
            pltpu.VMEM((2, FF, DM), BF),
            pltpu.VMEM((2, 8 * CAP, DM), BF),
            pltpu.VMEM((8 * CAP, FF), BF),
            pltpu.VMEM((8, 128, DM), BF),
            pltpu.VMEM((8, 128, 128), BF),
            pltpu.VMEM((8, 128, 128), F32),
            pltpu.SemaphoreType.DMA((6,)),
        ],
        cost_estimate=pl.CostEstimate(flops=8 * 10**9, bytes_accessed=28 * 10**6, transcendentals=10**6),
        name="experts",
    )(
        tab,
        meta_row,
        meta_col,
        *tokens,
        gate_weight[0],
        up_weight[0],
        down_weight[0],
        *expert_other,
    )
    by_off = {off: partial[2 * n : 2 * n + 2] for n, off in enumerate(ZREL)}

    def add(a, b):
        return (a.astype(F32) + b.astype(F32)).astype(BF)

    def back_along(j, sign, far):
        total = by_off[far if far == 4 else sign * far][j]
        for off in range(far - 1, 0, -1):
            total = add(shift_z(total, sign), by_off[sign * off][j])
        return shift_z(total, sign)

    halves = []
    for j in range(2):
        from_left = back_along(j, 1, 4 if j == 0 else 3)
        from_right = back_along(j, -1, 3 if j == 0 else 4)
        base = thinker_in[:, j * HALF : (j + 1) * HALF].astype(F32)
        total = base + by_off[0][j].astype(F32) + from_left.astype(F32) + from_right.astype(F32)
        halves.append(total.astype(BF))
    return jnp.concatenate(halves, axis=1)[None]


def solution(mesh):
    torus = Mesh(mesh.devices.reshape(NY, NX, NZ, 2), ALL)
    in_specs = (
        P(GRP, SEQ, None),
        P(GRP, SEQ),
        P(),
        P(None, GRP),
        P(None, GRP),
        P(None, GRP),
        P(),
        P(SEQ, None, None),
        P(SEQ, None, None),
        P(SEQ, None, None),
        P(GRP, SEQ, None),
        P(GRP, SEQ, None),
    )
    out_specs = P(GRP, SEQ, None)
    return jax.shard_map(body, mesh=torus, in_specs=in_specs, out_specs=out_specs, check_vma=False)
```

```python
import functools

import jax
import jax.numpy as jnp
from jax import lax
from jax.experimental import pallas as pl
from jax.experimental.pallas import tpu as pltpu
from jax.sharding import Mesh
from jax.sharding import PartitionSpec as P

HEADS = 20
HEAD = 64
D = 1280
DM = 2048
FF = 768
CAP = 48
GRP = ("y", "x")
SEQ = ("z", "core")
ALL = ("y", "x", "z", "core")
NY, NX, NZ = 4, 4, 8
LN_EPSILON = 1e-05
RMS_EPSILON = 1e-06
MASKED = -1e30
BF = jnp.bfloat16
F32 = jnp.float32

REL = (0, -1, 1, 2)
ZREL = (0, -1, 1, -2, 2, -3, 3, 4)
HALF = DM // 2


def flat(y, x, z, c):
    return (((y % NY) * NX + x % NX) * NZ + z % NZ) * 2 + c


def grp_perm(phase, sign):
    pairs = []
    for y in range(NY):
        for x in range(NX):
            for z in range(NZ):
                for c in range(2):
                    along_x = (c == 0) == (phase == 0)
                    dst = flat(y, x + sign, z, c) if along_x else flat(y + sign, x, z, c)
                    pairs.append((flat(y, x, z, c), dst))
    return pairs


def swap_cores(value):
    return lax.ppermute(value, "core", [(0, 1), (1, 0)])


def shift_z(value, sign):
    return lax.ppermute(value, "z", [(i, (i + sign) % NZ) for i in range(NZ)])


def join(*values):
    return lax.optimization_barrier(values)


def ring_step(first, second, phase):
    move = functools.partial(lax.ppermute, axis_name=ALL)
    return move(first, perm=grp_perm(phase, 1)), move(second, perm=grp_perm(phase, -1))


def layer_norm(signal, gain):
    widened = signal.astype(F32)
    average = jnp.mean(widened, axis=-1, keepdims=True)
    centred = widened - average
    variance = jnp.mean(centred * centred, axis=-1, keepdims=True)
    return centred * lax.rsqrt(variance + LN_EPSILON) * gain


def nn(a, b):
    return lax.dot_general(a, b, (((1,), (0,)), ((), ())), preferred_element_type=F32)


def load_pieces(tab, pieces, place, sems):
    copies = []
    for side in range(2):
        for p in range(4):
            for i in range(4):
                if p == 3:
                    src = pieces[side * 5 + 3 + i // 2].at[i % 2]
                else:
                    src = pieces[side * 5 + p].at[i]
                slot = p * 4 + i
                copy = pltpu.make_async_copy(
                    src, place(side, slot, tab[2 + side * 16 + slot]), sems.at[side * 16 + slot]
                )
                copy.start()
                copies.append(copy)
    return copies


def project_kernel(tab, nt, *refs):
    pieces, (qkv, w, sems) = refs[:10], refs[10:]
    core = tab[0]
    copies = load_pieces(
        tab, pieces, lambda side, slot, g: w.at[side, pl.ds(pl.multiple_of(g * 240, 16), 240), :], sems
    )
    for copy in copies:
        copy.wait()
    own = pl.ds(pl.multiple_of(core * 640, 128), 640)
    oth = pl.ds(pl.multiple_of(640 - core * 640, 128), 640)

    def query_rows(m, carry):
        rows = pl.ds(pl.multiple_of(m * 640, 128), 640)
        acc = nn(w[0, rows, :], nt[own, 0:256]) + nn(w[1, rows, :], nt[oth, 0:256])
        qkv[rows, 0:256] = acc.astype(BF) * BF(HEAD**-0.5)
        return carry

    def pair_rows(m, carry):
        rows = pl.ds(pl.multiple_of(m * 640, 128), 640)
        acc = nn(w[0, rows, :], nt[own, :]) + nn(w[1, rows, :], nt[oth, :])
        qkv[rows, :] = acc.astype(BF)
        return carry

    lax.fori_loop(0, 2, query_rows, 0)
    lax.fori_loop(2, 6, pair_rows, 0)


def heads_kernel(first, count, qkv, idk, idq, out, bias):
    bias[...] = jnp.where(idk[...] == idq[...], 0.0, MASKED)

    def one_head(h):
        base = (first + h) * HEAD
        q = qkv[pl.ds(pl.multiple_of(base, 64), HEAD), 0:256]
        k = qkv[pl.ds(pl.multiple_of(D + base, 64), HEAD), :]
        v = qkv[pl.ds(pl.multiple_of(2 * D + base, 64), HEAD), :]
        s = nn(k.T, q) + bias[...]
        top = jnp.max(s, axis=0, keepdims=True)
        e = jnp.exp(s - top)
        total = jnp.sum(e, axis=0, keepdims=True)
        o = nn(v, e.astype(BF)) / total
        out[pl.ds(pl.multiple_of(h * HEAD, 64), HEAD), :] = o.astype(BF)

    def pair(n, carry):
        one_head(2 * n)
        one_head(2 * n + 1)
        return carry

    lax.fori_loop(0, count // 2, pair, 0)


def tail_kernel(tab, att0, att1, audio_t, gain, *refs):
    pieces = refs[:10]
    thinker, x0, x1, w, wo, enc_t, acc, sems = refs[10:]
    core = tab[0]
    copies = load_pieces(tab, pieces, lambda side, slot, g: w.at[side, slot], sems)
    for side in range(2):
        for s in range(16):
            copies[side * 16 + s].wait()
            row = pl.multiple_of(tab[2 + side * 16 + s] * 80, 16)
            half = core if side == 0 else 1 - core
            for k in range(5):
                wo[half, pl.ds(row, 80), k * 128 : (k + 1) * 128] = w[side, s, k * 80 : (k + 1) * 80, :]

    def project(m, carry):
        rows = pl.ds(pl.multiple_of(m * 640, 128), 640)
        projected = nn(wo[0, rows, :], att0[...]) + nn(wo[1, rows, :], att1[...])
        enc_t[rows, :] = (audio_t[rows, :].astype(F32) + projected).astype(BF)
        return carry

    lax.fori_loop(0, 2, project, 0)
    even = enc_t[:, 0:128].T
    odd = enc_t[:, 128:256].T
    first = core == 0
    mine = jnp.where(first, even, odd)
    rest = jnp.where(first, odd, even)

    def columns(n, carry):
        p, i = n // 2, n % 2
        s, t = p * 4 + 2 * i, 8 * i + p
        both = jnp.concatenate([w[0, s, 400:1680, :], w[0, s + 1, 400:1680, :]], axis=1)
        block = nn(mine, both)
        both = jnp.concatenate([w[1, t, 400:1680, :], w[1, t + 4, 400:1680, :]], axis=1)
        block = block + nn(rest, both)
        acc[:, pl.ds(pl.multiple_of(tab[2 + s] * 128, 128), 128)] = block[:, :128]
        acc[:, pl.ds(pl.multiple_of(tab[3 + s] * 128, 128), 128)] = block[:, 128:]
        return carry

    lax.fori_loop(0, 8, columns, 0)
    rounded = acc[...].astype(BF)
    thinker[...] = rounded
    widened = rounded.astype(F32)
    squares = jnp.mean(widened * widened, axis=1, keepdims=True)
    normed = (widened * lax.rsqrt(squares + RMS_EPSILON) * gain[...]).astype(BF)
    x0[...] = normed[:, :HALF]
    x1[...] = normed[:, HALF:]


def expert_kernel(zrel, tab, meta_row, meta_col, *refs):
    chips = len(zrel)
    rows_e = chips * CAP
    xs, weights = refs[: 2 * chips], refs[2 * chips : 2 * chips + 6]
    outs = refs[2 * chips + 6 : 4 * chips + 6]
    wg, wu, wd, xbuf, xg, hid, yg, dsel, share, obuf, wsem, xsem, osem = refs[4 * chips + 6 :]
    core, z = tab[0], tab[1]

    def half(buf, r, j):
        return buf.at[r, :, j * HALF : (j + 1) * HALF]

    for r in range(chips):
        for j in range(2):
            pltpu.make_async_copy(xs[2 * r + j], half(xbuf, r, j), xsem.at[r, j]).start()
    copies = []
    for n, (src, dst) in enumerate(
        zip(weights, (wg.at[0], wu.at[0], wd.at[0], wg.at[1], wu.at[1], wd.at[1]))
    ):
        copy = pltpu.make_async_copy(src, dst, wsem.at[n])
        copy.start()
        copies.append(copy)
    e0 = (2 * z + core).astype(F32)
    e1 = (2 * z + 1 - core).astype(F32)
    lane = lax.broadcasted_iota(jnp.int32, (128, 128), 1)
    sub = lax.broadcasted_iota(jnp.int32, (128, 128), 0)
    lane_expert = jnp.where(lane < CAP, e0, e1)
    sub_expert = jnp.where(sub < CAP, e0, e1)
    lane_slot = jnp.where(lane < CAP, lane, lane - CAP).astype(F32)
    earlier = jnp.where(lane < sub, 1.0, 0.0).astype(BF)

    def choose(r, carry):
        off = jnp.int32(zrel[0])
        for n in range(1, chips):
            off = jnp.where(r == n, jnp.int32(zrel[n]), off)
        source = lax.rem(z + off + 8, 8)
        mc = meta_col[source]
        mr = meta_row[source]
        chosen = jnp.zeros((128, 128), F32)
        weight = jnp.zeros((128, 128), F32)
        for k in range(4):
            chosen = jnp.where(mc[:, k : k + 1] == lane_expert, 1.0, chosen)
            weight = jnp.where(mr[k : k + 1, :] == sub_expert, mr[4 + k : 5 + k, :], weight)
        place = nn(earlier, chosen.astype(BF))
        scatter = jnp.where((place == lane_slot) & (lane < 2 * CAP), chosen, 0.0)
        select = scatter.T
        dsel[r] = scatter.astype(BF)
        share[r] = jnp.broadcast_to(jnp.sum(select * weight, axis=1, keepdims=True), (128, 128))
        pick = select[: 2 * CAP].astype(BF)
        at = pl.ds(pl.multiple_of(r * CAP, 16), CAP)
        for j in range(2):
            pltpu.make_async_copy(xs[j], half(xbuf, r, j), xsem.at[r, j]).wait()
            rows = nn(pick, xbuf[r, :, j * HALF : (j + 1) * HALF]).astype(BF)
            xg[0, at, j * HALF : (j + 1) * HALF] = rows[:CAP]
            xg[1, at, j * HALF : (j + 1) * HALF] = rows[CAP:]
        yg[r, 2 * CAP :, :] = jnp.zeros((128 - 2 * CAP, DM), BF)
        return carry

    lax.fori_loop(0, chips, choose, 0)
    for e in range(2):
        copies[3 * e].wait()
        copies[3 * e + 1].wait()

        def up(n, carry):
            cols = pl.ds(pl.multiple_of(n * 256, 256), 256)
            gate_act = nn(xg[e], wg[e, :, cols])
            up_act = nn(xg[e], wu[e, :, cols])
            hid[:, cols] = (gate_act / (1.0 + jnp.exp(-gate_act)) * up_act).astype(BF)
            return carry

        lax.fori_loop(0, FF // 256, up, 0)
        copies[3 * e + 2].wait()

        def down(n, carry):
            cols = pl.ds(pl.multiple_of(n * 256, 256), 256)
            made = nn(hid[...], wd[e, :, cols])
            for r in range(chips):
                scale = share[r, e * CAP : (e + 1) * CAP, 0:1]
                yg[r, e * CAP : (e + 1) * CAP, cols] = (
                    made[r * CAP : (r + 1) * CAP] * scale
                ).astype(BF)
            return carry

        lax.fori_loop(0, DM // 256, down, 0)

    def spread(r, carry):
        for j in range(2):
            obuf[r, :, j * HALF : (j + 1) * HALF] = nn(
                dsel[r], yg[r, :, j * HALF : (j + 1) * HALF]
            ).astype(BF)
        return carry

    lax.fori_loop(0, chips, spread, 0)
    sends = []
    for r in range(chips):
        for j in range(2):
            copy = pltpu.make_async_copy(half(obuf, r, j), outs[2 * r + j], osem.at[r, j])
            copy.start()
            sends.append(copy)
    for copy in sends:
        copy.wait()


VMEM = pl.BlockSpec(memory_space=pltpu.VMEM)
SMEM = pl.BlockSpec(memory_space=pltpu.SMEM)
ANY = pl.BlockSpec(memory_space=pl.ANY)


def shape(*dims, dtype=BF):
    return jax.ShapeDtypeStruct(dims, dtype)


def body(
    audio,
    block_ids,
    norm_gain,
    qkv_weight,
    out_weight,
    adapter_weight,
    moe_gain,
    gate_weight,
    up_weight,
    down_weight,
    routes,
    route_weights,
):
    y, x = lax.axis_index("y"), lax.axis_index("x")
    z, core = lax.axis_index("z"), lax.axis_index("core")

    count = NZ * 2
    ahead = [(i, i + 1) for i in range(count - 1)]
    back = [(i + 1, i) for i in range(count - 1)]
    signal = audio[0]
    ids = block_ids[0].astype(F32)
    weights_here = route_weights[0]
    shares = weights_here / jnp.sum(weights_here, axis=1, keepdims=True)
    meta = jnp.concatenate(
        [routes[0].astype(F32).T, shares.T, ids.reshape(2, 128), jnp.zeros((6, 128), F32)]
    )
    mine = lax.dynamic_slice_in_dim(qkv_weight.T, core * 640, 640, 1)
    a, b = join(*ring_step(mine, mine, 0))
    o0, o1, left, right, signal, meta = join(
        *ring_step(a[:128], b[128:], 0),
        lax.ppermute(signal[128:], SEQ, ahead),
        lax.ppermute(signal[:128], SEQ, back),
        signal,
        meta,
    )
    block = jnp.stack([mine, a, b, jnp.concatenate([o0, o1])])

    paired = signal.reshape(128, 2, D)
    extended = jnp.concatenate([paired[:, 0], paired[:, 1], left, right])
    normed_t = layer_norm(extended, norm_gain).astype(BF).T
    audio_t = extended[:256].T
    meta_all = lax.all_to_all(
        jnp.broadcast_to(meta[None], (count, 16, 128)), SEQ, split_axis=0, concat_axis=0, tiled=True
    )

    out_t = lax.dynamic_slice_in_dim(out_weight.T, core * 640, 640, 1)
    out_t = out_t.reshape(80, 5, 128).transpose(1, 0, 2).reshape(400, 128)
    ada = lax.dynamic_slice_in_dim(adapter_weight, core * D, D, 0)
    oa_mine = jnp.concatenate([out_t, ada])
    oa_mine = join(oa_mine, o0)[0]
    qa, qb, a, b, s_own, normed_t, audio_t, meta_all = join(
        *ring_step(block, block, 1),
        *ring_step(oa_mine, oa_mine, 0),
        swap_cores(block),
        normed_t,
        audio_t,
        meta_all,
    )
    mates = lax.dynamic_index_in_dim(meta_all.reshape(NZ, 2, 16, 128), core, 1, keepdims=False)
    meta_row = mates[:, :8]
    meta_col = meta_row.transpose(0, 2, 1)
    seq = z * 2 + core
    ids_left = lax.dynamic_index_in_dim(meta_all, jnp.maximum(seq - 1, 0), 0, keepdims=False)[9]
    ids_right = lax.dynamic_index_in_dim(meta_all, jnp.minimum(seq + 1, count - 1), 0, keepdims=False)[8]
    ids_left = jnp.where(seq > 0, ids_left, -1.0)
    ids_right = jnp.where(seq < count - 1, ids_right, -1.0)
    ids_paired = ids.reshape(128, 2)
    ids_all = jnp.concatenate([ids_paired[:, 0], ids_paired[:, 1], ids_left, ids_right])
    qo0, qo1, o0, o1, s_a, s_b, meta_row, meta_col, ids_all = join(
        *ring_step(qa[:2], qb[2:], 1),
        *ring_step(a[:848], b[848:], 0),
        swap_cores(qa),
        swap_cores(qb),
        meta_row,
        meta_col,
        ids_all,
    )
    oa_block = jnp.stack([oa_mine, a, b, jnp.concatenate([o0, o1])])
    qkv_own = (block, qa, qb, qo0, qo1)
    qkv_other = (s_own, s_a, s_b, swap_cores(qo0), swap_cores(qo1))
    oa_a, oa_b = ring_step(oa_block, oa_block, 1)
    oa_s = swap_cores(oa_block)

    rel = jnp.array(REL, jnp.int32)
    at_y, at_x = (y + rel) % NY, (x + rel) % NX
    table0 = at_y[:, None] * NX + at_x[None, :]
    table1 = at_y[None, :] * NX + at_x[:, None]
    own_table = jnp.where(core == 0, table0, table1).reshape(-1)
    other_table = jnp.where(core == 0, table1, table0).reshape(-1)
    tab = jnp.concatenate([jnp.stack([core, z]), own_table, other_table]).astype(jnp.int32)

    qkv = pl.pallas_call(
        project_kernel,
        out_shape=shape(3 * D, 512),
        in_specs=[SMEM, VMEM] + [ANY] * 10,
        out_specs=VMEM,
        scratch_shapes=[pltpu.VMEM((2, 3 * D, 640), BF), pltpu.SemaphoreType.DMA((32,))],
        compiler_params=pltpu.CompilerParams(vmem_limit_bytes=24 << 20),
        cost_estimate=pl.CostEstimate(flops=5 * 10**9, bytes_accessed=15 * 10**6, transcendentals=0),
        name="project",
    )(tab, normed_t, *qkv_own, *qkv_other)

    def attend(qkv, first_head):
        return pl.pallas_call(
            functools.partial(heads_kernel, first_head, HEADS // 2),
            out_shape=shape(D // 2, 256),
            in_specs=[VMEM] * 3,
            out_specs=VMEM,
            scratch_shapes=[pltpu.VMEM((512, 256), F32)],
            compiler_params=pltpu.CompilerParams(vmem_limit_bytes=16 << 20),
            cost_estimate=pl.CostEstimate(
                flops=5 * 10**9, bytes_accessed=4 * 10**6, transcendentals=10**6
            ),
            name="heads",
        )(qkv, ids_all[:, None], ids_all[None, :256])

    attended0 = attend(qkv, 0)
    attended0, qkv, oa_a, oa_b, oa_s = join(attended0, qkv, oa_a, oa_b, oa_s)
    attended1, oa_o0, oa_o1, oa_sa, oa_sb = join(
        attend(qkv, HEADS // 2),
        *ring_step(oa_a[:2], oa_b[2:], 1),
        swap_cores(oa_a),
        swap_cores(oa_b),
    )
    oa_so0, oa_so1 = join(swap_cores(oa_o0), swap_cores(oa_o1))
    attended = (attended0, attended1)
    oa_own = (oa_block, oa_a, oa_b, oa_o0, oa_o1)
    oa_other = (oa_s, oa_sa, oa_sb, oa_so0, oa_so1)
    own_expert = join(gate_weight[0], up_weight[0], down_weight[0], oa_so1)[:3]
    expert_other = [swap_cores(v) for v in own_expert]

    thinker_in, x0, x1 = pl.pallas_call(
        tail_kernel,
        out_shape=[shape(128, DM), shape(128, HALF), shape(128, HALF)],
        in_specs=[SMEM, VMEM, VMEM, VMEM, VMEM] + [ANY] * 10,
        out_specs=[VMEM] * 3,
        scratch_shapes=[
            pltpu.VMEM((2, 16, 1680, 128), BF),
            pltpu.VMEM((2, D, 640), BF),
            pltpu.VMEM((D, 256), BF),
            pltpu.VMEM((128, DM), F32),
            pltpu.SemaphoreType.DMA((32,)),
        ],
        compiler_params=pltpu.CompilerParams(vmem_limit_bytes=32 << 20),
        cost_estimate=pl.CostEstimate(flops=3 * 10**9, bytes_accessed=16 * 10**6, transcendentals=0),
        name="tail",
    )(tab, *attended, audio_t, moe_gain[None], *oa_own, *oa_other)

    up0, up1, down0, down1 = [x0], [x1], [x0], [x1]
    for step in range(4):
        up0.append(shift_z(up0[-1], 1))
        down1.append(shift_z(down1[-1], -1))
        if step < 3:
            up1.append(shift_z(up1[-1], 1))
            down0.append(shift_z(down0[-1], -1))

    def tokens_from(off):
        if off == 4:
            return [up0[4], down1[4]]
        return [up0[-off], up1[-off]] if off <= 0 else [down0[off], down1[off]]

    def experts(zrel):
        chips = len(zrel)
        return pl.pallas_call(
            functools.partial(expert_kernel, zrel),
            out_shape=[shape(128, HALF)] * (2 * chips),
            in_specs=[SMEM, VMEM, VMEM] + [ANY] * (2 * chips + 6),
            out_specs=[ANY] * (2 * chips),
            scratch_shapes=[
                pltpu.VMEM((2, DM, FF), BF),
                pltpu.VMEM((2, DM, FF), BF),
                pltpu.VMEM((2, FF, DM), BF),
                pltpu.VMEM((chips, 128, DM), BF),
                pltpu.VMEM((2, chips * CAP, DM), BF),
                pltpu.VMEM((chips * CAP, FF), BF),
                pltpu.VMEM((chips, 128, DM), BF),
                pltpu.VMEM((chips, 128, 128), BF),
                pltpu.VMEM((chips, 128, 128), F32),
                pltpu.VMEM((chips, 128, DM), BF),
                pltpu.SemaphoreType.DMA((6,)),
                pltpu.SemaphoreType.DMA((chips, 2)),
                pltpu.SemaphoreType.DMA((chips, 2)),
            ],
            compiler_params=pltpu.CompilerParams(vmem_limit_bytes=40 << 20),
            cost_estimate=pl.CostEstimate(
                flops=chips * 10**9, bytes_accessed=28 * 10**6, transcendentals=10**6
            ),
            name="experts",
        )(
            tab,
            meta_row,
            meta_col,
            *[v for off in zrel for v in tokens_from(off)],
            gate_weight[0],
            up_weight[0],
            down_weight[0],
            *expert_other,
        )

    by_off = {}
    for zrel in (ZREL[:5], ZREL[5:]):
        partial = experts(zrel)
        by_off.update({off: partial[2 * n : 2 * n + 2] for n, off in enumerate(zrel)})

    def add(a, b):
        return (a.astype(F32) + b.astype(F32)).astype(BF)

    def back_along(j, sign, far):
        total = by_off[far if far == 4 else sign * far][j]
        for off in range(far - 1, 0, -1):
            total = add(shift_z(total, sign), by_off[sign * off][j])
        return shift_z(total, sign)

    halves = []
    for j in range(2):
        from_left = back_along(j, 1, 4 if j == 0 else 3)
        from_right = back_along(j, -1, 3 if j == 0 else 4)
        base = thinker_in[:, j * HALF : (j + 1) * HALF].astype(F32)
        total = base + by_off[0][j].astype(F32) + from_left.astype(F32) + from_right.astype(F32)
        halves.append(total.astype(BF))
    return jnp.concatenate(halves, axis=1)[None]


def solution(mesh):
    torus = Mesh(mesh.devices.reshape(NY, NX, NZ, 2), ALL)
    in_specs = (
        P(GRP, SEQ, None),
        P(GRP, SEQ),
        P(),
        P(None, GRP),
        P(None, GRP),
        P(None, GRP),
        P(),
        P(SEQ, None, None),
        P(SEQ, None, None),
        P(SEQ, None, None),
        P(GRP, SEQ, None),
        P(GRP, SEQ, None),
    )
    out_specs = P(GRP, SEQ, None)
    return jax.shard_map(body, mesh=torus, in_specs=in_specs, out_specs=out_specs, check_vma=False)
```

```python
import functools

import jax
import jax.numpy as jnp
from jax import lax
from jax.experimental import pallas as pl
from jax.experimental.pallas import tpu as pltpu
from jax.sharding import Mesh
from jax.sharding import PartitionSpec as P


HEADS = 20
HEAD = 64
D = 1280
DM = 2048
FF = 768
CAP = 48
GRP = ("y", "x")
SEQ = ("z", "core")
ALL = ("y", "x", "z", "core")
NY, NX, NZ = 4, 4, 8
LN_EPSILON = 1e-05
RMS_EPSILON = 1e-06
MASKED = -1e30
BF = jnp.bfloat16
F32 = jnp.float32

REL = (0, -1, 1, 2)
ZREL = (0, -1, 1, -2, 2, -3, 3, 4)
HALF = DM // 2


def flat(y, x, z, c):
    return (((y % NY) * NX + x % NX) * NZ + z % NZ) * 2 + c


def grp_perm(phase, sign):
    pairs = []
    for y in range(NY):
        for x in range(NX):
            for z in range(NZ):
                for c in range(2):
                    along_x = (c == 0) == (phase == 0)
                    dst = flat(y, x + sign, z, c) if along_x else flat(y + sign, x, z, c)
                    pairs.append((flat(y, x, z, c), dst))
    return pairs


def swap_cores(value):
    return lax.ppermute(value, "core", [(0, 1), (1, 0)])


def shift_z(value, sign):
    return lax.ppermute(value, "z", [(i, (i + sign) % NZ) for i in range(NZ)])


def join(*values):
    return lax.optimization_barrier(values)


def ring_step(first, second, phase):
    move = functools.partial(lax.ppermute, axis_name=ALL)
    return move(first, perm=grp_perm(phase, 1)), move(second, perm=grp_perm(phase, -1))


def layer_norm(signal, gain):
    widened = signal.astype(F32)
    average = jnp.mean(widened, axis=-1, keepdims=True)
    centred = widened - average
    variance = jnp.mean(centred * centred, axis=-1, keepdims=True)
    return (centred * lax.rsqrt(variance + LN_EPSILON) * gain).astype(BF)


def nn(a, b):
    return lax.dot_general(a, b, (((1,), (0,)), ((), ())), preferred_element_type=F32)


def prep_kernel(own, left, right, ids, gain, nt, audio_t, idk, idq):
    frame = lax.broadcasted_iota(jnp.int32, (256, 256), 0)
    slot = lax.broadcasted_iota(jnp.int32, (256, 256), 1)
    order = jnp.where(slot < 128, 2 * slot, 2 * slot - 255)
    place = jnp.where(frame == order, 1.0, 0.0).astype(BF)
    nt[:, 0:256] = nn(layer_norm(own[...], gain[...]).T, place).astype(BF)
    nt[:, 256:384] = layer_norm(left[:128, :], gain[...]).T
    nt[:, 384:512] = layer_norm(right[:128, :], gain[...]).T
    audio_t[...] = nn(own[...].T, place).astype(BF)
    numbers = nn(ids[...].astype(BF), place)
    idq[...] = numbers
    tags = [numbers[0:1, :], left[128:136, 0:128].astype(F32)[0:1], right[128:136, 0:128].astype(F32)[0:1]]
    idk[...] = jnp.broadcast_to(jnp.concatenate(tags, axis=1), (128, 512)).T


def load_pieces(tab, pieces, place, sems):
    copies = []
    for side in range(2):
        for p in range(4):
            for i in range(4):
                if p == 3:
                    src = pieces[side * 5 + 3 + i // 2].at[i % 2]
                else:
                    src = pieces[side * 5 + p].at[i]
                slot = p * 4 + i
                copy = pltpu.make_async_copy(
                    src, place(side, slot, tab[2 + side * 16 + slot]), sems.at[side * 16 + slot]
                )
                copy.start()
                copies.append(copy)
    return copies


def project_kernel(tab, nt, *refs):
    pieces, (qkv, w, sems) = refs[:10], refs[10:]
    core = tab[0]
    copies = load_pieces(
        tab, pieces, lambda side, slot, g: w.at[side, pl.ds(pl.multiple_of(g * 240, 16), 240), :], sems
    )
    for copy in copies:
        copy.wait()
    own = pl.ds(pl.multiple_of(core * 640, 128), 640)
    oth = pl.ds(pl.multiple_of(640 - core * 640, 128), 640)

    def query_rows(m, carry):
        rows = pl.ds(pl.multiple_of(m * 640, 128), 640)
        acc = nn(w[0, rows, :], nt[own, 0:256]) + nn(w[1, rows, :], nt[oth, 0:256])
        qkv[rows, 0:256] = acc.astype(BF) * BF(HEAD**-0.5)
        return carry

    def pair_rows(m, carry):
        rows = pl.ds(pl.multiple_of(m * 640, 128), 640)
        acc = nn(w[0, rows, :], nt[own, :]) + nn(w[1, rows, :], nt[oth, :])
        qkv[rows, :] = acc.astype(BF)
        return carry

    lax.fori_loop(0, 2, query_rows, 0)
    lax.fori_loop(2, 6, pair_rows, 0)


def heads_kernel(first, count, qkv, idk, idq, out, bias):
    bias[...] = jnp.where(idk[:, 0:1] == idq[0:1, :], 0.0, MASKED)

    def one_head(h):
        base = (first + h) * HEAD
        q = qkv[pl.ds(pl.multiple_of(base, 64), HEAD), 0:256]
        k = qkv[pl.ds(pl.multiple_of(D + base, 64), HEAD), :]
        v = qkv[pl.ds(pl.multiple_of(2 * D + base, 64), HEAD), :]
        s = nn(k.T, q) + bias[...]
        top = jnp.max(s, axis=0, keepdims=True)
        e = jnp.exp(s - top)
        total = jnp.sum(e, axis=0, keepdims=True)
        o = nn(v, e.astype(BF)) / total
        out[pl.ds(pl.multiple_of(h * HEAD, 64), HEAD), :] = o.astype(BF)

    def pair(n, carry):
        one_head(2 * n)
        one_head(2 * n + 1)
        return carry

    lax.fori_loop(0, count // 2, pair, 0)


def tail_kernel(tab, att0, att1, audio_t, gain, meta, *refs):
    pieces = refs[:10]
    thinker, x0, x1, w, wo, enc_t, acc, rider, sems = refs[10:]
    core = tab[0]
    copies = load_pieces(tab, pieces, lambda side, slot, g: w.at[side, slot], sems)
    for side in range(2):
        for s in range(16):
            copies[side * 16 + s].wait()
            row = pl.multiple_of(tab[2 + side * 16 + s] * 80, 16)
            half = core if side == 0 else 1 - core
            for k in range(5):
                wo[half, pl.ds(row, 80), k * 128 : (k + 1) * 128] = w[side, s, k * 80 : (k + 1) * 80, :]

    def project(m, carry):
        rows = pl.ds(pl.multiple_of(m * 640, 128), 640)
        projected = nn(wo[0, rows, :], att0[...]) + nn(wo[1, rows, :], att1[...])
        enc_t[rows, :] = (audio_t[rows, :].astype(F32) + projected).astype(BF)
        return carry

    lax.fori_loop(0, 2, project, 0)
    even = enc_t[:, 0:128].T
    odd = enc_t[:, 128:256].T
    first = core == 0
    mine = jnp.where(first, even, odd)
    rest = jnp.where(first, odd, even)

    def columns(n, carry):
        p, i = n // 2, n % 2
        s, t = p * 4 + 2 * i, 8 * i + p
        both = jnp.concatenate([w[0, s, 400:1680, :], w[0, s + 1, 400:1680, :]], axis=1)
        block = nn(mine, both)
        both = jnp.concatenate([w[1, t, 400:1680, :], w[1, t + 4, 400:1680, :]], axis=1)
        block = block + nn(rest, both)
        acc[:, pl.ds(pl.multiple_of(tab[2 + s] * 128, 128), 128)] = block[:, :128]
        acc[:, pl.ds(pl.multiple_of(tab[3 + s] * 128, 128), 128)] = block[:, 128:]
        return carry

    lax.fori_loop(0, 8, columns, 0)
    rounded = acc[...].astype(BF)
    thinker[...] = rounded
    widened = rounded.astype(F32)
    squares = jnp.mean(widened * widened, axis=1, keepdims=True)
    normed = (widened * lax.rsqrt(squares + RMS_EPSILON) * gain[...]).astype(BF)
    x0[0:128, :] = normed[:, :HALF]
    rider[...] = jnp.zeros((8, HALF), F32)
    for k in range(4):
        one = slice(k * 128, (k + 1) * 128)
        two = slice(512 + k * 128, 512 + (k + 1) * 128)
        share = meta[4 + k : 5 + k, :]
        high = share.astype(BF).astype(F32)
        middle = (share - high).astype(BF).astype(F32)
        rider[0:1, one] = meta[k : k + 1, :]
        rider[0:1, two] = high
        rider[1:2, one] = middle
        rider[1:2, two] = share - high - middle
    x0[128:136, :] = rider[...].astype(BF)
    x1[...] = normed[:, HALF:]


def expert_kernel(tab, *refs):
    xs, weights = refs[:16], refs[16:22]
    outs = refs[22:38]
    wg, wu, wd, xg, hid, yg, dsel, share, sems = refs[38:]
    core, z = tab[0], tab[1]
    copies = []
    for n, (src, dst) in enumerate(
        zip(weights, (wg.at[0], wu.at[0], wd.at[0], wg.at[1], wu.at[1], wd.at[1]))
    ):
        copy = pltpu.make_async_copy(src, dst, sems.at[n])
        copy.start()
        copies.append(copy)
    e0 = (2 * z + core).astype(F32)
    e1 = (2 * z + 1 - core).astype(F32)
    lane = lax.broadcasted_iota(jnp.int32, (128, 128), 1)
    sub = lax.broadcasted_iota(jnp.int32, (128, 128), 0)
    expert = jnp.where(sub < CAP, e0, e1)
    slot = jnp.where(sub < CAP, sub, sub - CAP).astype(F32)
    earlier = jnp.where(sub < lane, 1.0, 0.0).astype(BF)
    for r in range(8):
        rider = xs[2 * r][128:136, :].astype(F32)
        chosen = jnp.zeros((128, 128), F32)
        weight = jnp.zeros((128, 128), F32)
        for k in range(4):
            one = slice(k * 128, (k + 1) * 128)
            two = slice(512 + k * 128, 512 + (k + 1) * 128)
            hit = rider[0:1, one] == expert
            chosen = jnp.where(hit, 1.0, chosen)
            weight = jnp.where(hit, rider[0:1, two] + rider[1:2, one] + rider[1:2, two], weight)
        place = nn(chosen.astype(BF), earlier)
        select = jnp.where((place == slot) & (sub < 2 * CAP), chosen, 0.0)
        dsel[r] = select.T.astype(BF)
        share[r] = jnp.broadcast_to(jnp.sum(select * weight, axis=1, keepdims=True), (128, 128))
        pick = select[: 2 * CAP].astype(BF)
        for j in range(2):
            rows = nn(pick, xs[2 * r + j][0:128, :]).astype(BF)
            xg[0, r * CAP : (r + 1) * CAP, j * HALF : (j + 1) * HALF] = rows[:CAP]
            xg[1, r * CAP : (r + 1) * CAP, j * HALF : (j + 1) * HALF] = rows[CAP:]
        yg[r, 2 * CAP :, :] = jnp.zeros((128 - 2 * CAP, DM), BF)
    for e in range(2):
        copies[3 * e].wait()
        copies[3 * e + 1].wait()

        def up(n, carry):
            cols = pl.ds(pl.multiple_of(n * 256, 256), 256)
            gate_act = nn(xg[e], wg[e, :, cols])
            up_act = nn(xg[e], wu[e, :, cols])
            hid[:, cols] = (gate_act / (1.0 + jnp.exp(-gate_act)) * up_act).astype(BF)
            return carry

        lax.fori_loop(0, FF // 256, up, 0)
        copies[3 * e + 2].wait()

        def down(n, carry):
            cols = pl.ds(pl.multiple_of(n * 256, 256), 256)
            made = nn(hid[...], wd[e, :, cols])
            for r in range(8):
                scale = share[r, e * CAP : (e + 1) * CAP, 0:1]
                yg[r, e * CAP : (e + 1) * CAP, cols] = (
                    made[r * CAP : (r + 1) * CAP] * scale
                ).astype(BF)
            return carry

        lax.fori_loop(0, DM // 256, down, 0)
    for r in range(8):
        for j in range(2):
            outs[2 * r + j][...] = nn(dsel[r], yg[r, :, j * HALF : (j + 1) * HALF]).astype(BF)


VMEM = pl.BlockSpec(memory_space=pltpu.VMEM)
SMEM = pl.BlockSpec(memory_space=pltpu.SMEM)
ANY = pl.BlockSpec(memory_space=pl.ANY)


def shape(*dims, dtype=BF):
    return jax.ShapeDtypeStruct(dims, dtype)


def layer(
    audio,
    block_ids,
    norm_gain,
    qkv_weight,
    out_weight,
    adapter_weight,
    moe_gain,
    gate_weight,
    up_weight,
    down_weight,
    routes,
    route_weights,
):
    y, x = lax.axis_index("y"), lax.axis_index("x")
    z, core = lax.axis_index("z"), lax.axis_index("core")

    count = NZ * 2
    ahead = [(i, i + 1) for i in range(count - 1)]
    back = [(i + 1, i) for i in range(count - 1)]
    signal = audio[0]
    weights_here = route_weights[0]
    shares = weights_here / jnp.sum(weights_here, axis=1, keepdims=True)
    meta = jnp.concatenate([routes[0].astype(F32).T, shares.T])
    tags = (block_ids[0] + 1).astype(F32)
    rider = jnp.pad(tags.astype(BF).reshape(2, 1, 128), ((0, 0), (0, 7), (0, 1280 - 128)))
    to_right = jnp.concatenate([signal[128:], rider[1]])
    to_left = jnp.concatenate([signal[:128], rider[0]])
    mine = lax.dynamic_slice_in_dim(qkv_weight.T, core * 640, 640, 1)
    a, b = join(*ring_step(mine, mine, 0))
    o0, o1, left, right = join(
        *ring_step(a[:128], b[128:], 0),
        lax.ppermute(to_right, SEQ, ahead),
        lax.ppermute(to_left, SEQ, back),
    )
    block = jnp.stack([mine, a, b, jnp.concatenate([o0, o1])])

    normed_t, audio_t, idk, idq = pl.pallas_call(
        prep_kernel,
        out_shape=[
            shape(D, 512),
            shape(D, 256),
            shape(512, 128, dtype=F32),
            shape(8, 256, dtype=F32),
        ],
        in_specs=[VMEM] * 5,
        out_specs=[VMEM] * 4,
        cost_estimate=pl.CostEstimate(flops=10**9, bytes_accessed=4 * 10**6, transcendentals=0),
        name="prep",
    )(signal, left, right, jnp.broadcast_to(tags[None], (8, 256)), norm_gain[None])

    out_t = lax.dynamic_slice_in_dim(out_weight.T, core * 640, 640, 1)
    out_t = out_t.reshape(80, 5, 128).transpose(1, 0, 2).reshape(400, 128)
    ada = lax.dynamic_slice_in_dim(adapter_weight, core * D, D, 0)
    oa_mine = jnp.concatenate([out_t, ada])
    oa_mine = join(oa_mine, o0)[0]
    qa, qb, a, b, s_own, normed_t, audio_t, idk, idq, meta = join(
        *ring_step(block, block, 1),
        *ring_step(oa_mine, oa_mine, 0),
        swap_cores(block),
        normed_t,
        audio_t,
        idk,
        idq,
        meta,
    )
    far = ring_step(qa[:2], qb[2:], 1)
    swaps = swap_cores(qa), swap_cores(qb)
    qo0, qo1, o0, o1, s_a, s_b = join(*far, *ring_step(a[:848], b[848:], 0), *swaps)
    oa_block = jnp.stack([oa_mine, a, b, jnp.concatenate([o0, o1])])
    qkv_own = (block, qa, qb, qo0, qo1)
    qkv_other = (s_own, s_a, s_b, swap_cores(qo0), swap_cores(qo1))
    oa_a, oa_b = ring_step(oa_block, oa_block, 1)
    oa_s = swap_cores(oa_block)

    rel = jnp.array(REL, jnp.int32)
    at_y, at_x = (y + rel) % NY, (x + rel) % NX
    table0 = at_y[:, None] * NX + at_x[None, :]
    table1 = at_y[None, :] * NX + at_x[:, None]
    own_table = jnp.where(core == 0, table0, table1).reshape(-1)
    other_table = jnp.where(core == 0, table1, table0).reshape(-1)
    tab = jnp.concatenate([jnp.stack([core, z]), own_table, other_table]).astype(jnp.int32)

    qkv = pl.pallas_call(
        project_kernel,
        out_shape=shape(3 * D, 512),
        in_specs=[SMEM, VMEM] + [ANY] * 10,
        out_specs=VMEM,
        scratch_shapes=[pltpu.VMEM((2, 3 * D, 640), BF), pltpu.SemaphoreType.DMA((32,))],
        cost_estimate=pl.CostEstimate(flops=5 * 10**9, bytes_accessed=15 * 10**6, transcendentals=0),
        name="project",
    )(tab, normed_t, *qkv_own, *qkv_other)

    def attend(qkv, first_head):
        return pl.pallas_call(
            functools.partial(heads_kernel, first_head, HEADS // 2),
            out_shape=shape(D // 2, 256),
            in_specs=[VMEM] * 3,
            out_specs=VMEM,
            scratch_shapes=[pltpu.VMEM((512, 256), F32)],
                cost_estimate=pl.CostEstimate(
                flops=5 * 10**9, bytes_accessed=4 * 10**6, transcendentals=10**6
            ),
            name="heads",
        )(qkv, idk, idq)

    attended0 = attend(qkv, 0)
    attended0, qkv, oa_a, oa_b, oa_s = join(attended0, qkv, oa_a, oa_b, oa_s)
    far = ring_step(oa_a[:2], oa_b[2:], 1)
    swaps = swap_cores(oa_a), swap_cores(oa_b)
    attended1, oa_o0, oa_o1, oa_sa, oa_sb = join(attend(qkv, HEADS // 2), *far, *swaps)
    oa_so0, oa_so1 = join(swap_cores(oa_o0), swap_cores(oa_o1))
    attended = (attended0, attended1)
    oa_own = (oa_block, oa_a, oa_b, oa_o0, oa_o1)
    oa_other = (oa_s, oa_sa, oa_sb, oa_so0, oa_so1)
    own_expert = join(gate_weight[0], up_weight[0], down_weight[0], oa_so1)[:3]
    expert_other = [swap_cores(v) for v in own_expert]

    thinker_in, x0, x1 = pl.pallas_call(
        tail_kernel,
        out_shape=[shape(128, DM), shape(136, HALF), shape(128, HALF)],
        in_specs=[SMEM, VMEM, VMEM, VMEM, VMEM, VMEM] + [ANY] * 10,
        out_specs=[VMEM] * 3,
        scratch_shapes=[
            pltpu.VMEM((2, 16, 1680, 128), BF),
            pltpu.VMEM((2, D, 640), BF),
            pltpu.VMEM((D, 256), BF),
            pltpu.VMEM((128, DM), F32),
            pltpu.VMEM((8, HALF), F32),
            pltpu.SemaphoreType.DMA((32,)),
        ],
        cost_estimate=pl.CostEstimate(flops=3 * 10**9, bytes_accessed=16 * 10**6, transcendentals=0),
        name="tail",
    )(tab, *attended, audio_t, moe_gain[None], meta, *oa_own, *oa_other)

    up0, up1, down0, down1 = [x0], [x1], [x0], [x1]
    for step in range(4):
        up0.append(shift_z(up0[-1], 1))
        down1.append(shift_z(down1[-1], -1))
        if step < 3:
            up1.append(shift_z(up1[-1], 1))
            down0.append(shift_z(down0[-1], -1))

    def tokens_from(off):
        if off == 4:
            return [up0[4], down1[4]]
        return [up0[-off], up1[-off]] if off <= 0 else [down0[off], down1[off]]

    partial = pl.pallas_call(
        expert_kernel,
        out_shape=[shape(128, HALF)] * 16,
        in_specs=[SMEM] + [VMEM] * 16 + [ANY] * 6,
        out_specs=[VMEM] * 16,
        scratch_shapes=[
            pltpu.VMEM((2, DM, FF), BF),
            pltpu.VMEM((2, DM, FF), BF),
            pltpu.VMEM((2, FF, DM), BF),
            pltpu.VMEM((2, 8 * CAP, DM), BF),
            pltpu.VMEM((8 * CAP, FF), BF),
            pltpu.VMEM((8, 128, DM), BF),
            pltpu.VMEM((8, 128, 128), BF),
            pltpu.VMEM((8, 128, 128), F32),
            pltpu.SemaphoreType.DMA((6,)),
        ],
        cost_estimate=pl.CostEstimate(
            flops=8 * 10**9, bytes_accessed=28 * 10**6, transcendentals=10**6
        ),
        name="experts",
    )(
        tab,
        *[v for off in ZREL for v in tokens_from(off)],
        gate_weight[0],
        up_weight[0],
        down_weight[0],
        *expert_other,
    )
    by_off = {off: partial[2 * n : 2 * n + 2] for n, off in enumerate(ZREL)}

    def add(a, b):
        return (a.astype(F32) + b.astype(F32)).astype(BF)

    def back_along(j, sign, far):
        total = by_off[far if far == 4 else sign * far][j]
        for off in range(far - 1, 0, -1):
            total = add(shift_z(total, sign), by_off[sign * off][j])
        return shift_z(total, sign)

    halves = []
    for j in range(2):
        from_left = back_along(j, 1, 4 if j == 0 else 3)
        from_right = back_along(j, -1, 3 if j == 0 else 4)
        base = thinker_in[:, j * HALF : (j + 1) * HALF].astype(F32)
        total = base + by_off[0][j].astype(F32) + from_left.astype(F32) + from_right.astype(F32)
        halves.append(total.astype(BF))
    return jnp.concatenate(halves, axis=1)[None]


def solution(mesh):
    torus = Mesh(mesh.devices.reshape(NY, NX, NZ, 2), ALL)
    in_specs = (
        P(GRP, SEQ, None),
        P(GRP, SEQ),
        P(),
        P(None, GRP),
        P(None, GRP),
        P(None, GRP),
        P(),
        P(SEQ, None, None),
        P(SEQ, None, None),
        P(SEQ, None, None),
        P(GRP, SEQ, None),
        P(GRP, SEQ, None),
    )
    out_specs = P(GRP, SEQ, None)
    return jax.shard_map(layer, mesh=torus, in_specs=in_specs, out_specs=out_specs, check_vma=False)
```

```python
import functools

import jax
import jax.numpy as jnp
from jax import lax
from jax.experimental import pallas as pl
from jax.experimental.pallas import tpu as pltpu
from jax.sharding import Mesh
from jax.sharding import PartitionSpec as P


HEADS = 20
HEAD = 64
D = 1280
DM = 2048
FF = 768
CAP = 48
GRP = ("y", "x")
SEQ = ("z", "core")
ALL = ("y", "x", "z", "core")
NY, NX, NZ = 4, 4, 8
LN_EPSILON = 1e-05
RMS_EPSILON = 1e-06
MASKED = -1e30
BF = jnp.bfloat16
F32 = jnp.float32

REL = (0, -1, 1, 2)
ZREL = (0, -1, 1, -2, 2, -3, 3, 4)
HALF = DM // 2


def flat(y, x, z, c):
    return (((y % NY) * NX + x % NX) * NZ + z % NZ) * 2 + c


def grp_perm(phase, sign):
    pairs = []
    for y in range(NY):
        for x in range(NX):
            for z in range(NZ):
                for c in range(2):
                    along_x = (c == 0) == (phase == 0)
                    dst = flat(y, x + sign, z, c) if along_x else flat(y + sign, x, z, c)
                    pairs.append((flat(y, x, z, c), dst))
    return pairs


def swap_cores(value):
    return lax.ppermute(value, "core", [(0, 1), (1, 0)])


def shift_z(value, sign):
    return lax.ppermute(value, "z", [(i, (i + sign) % NZ) for i in range(NZ)])


def join(*values):
    return lax.optimization_barrier(values)


def ring_step(first, second, phase):
    move = functools.partial(lax.ppermute, axis_name=ALL)
    return move(first, perm=grp_perm(phase, 1)), move(second, perm=grp_perm(phase, -1))


def layer_norm(signal, gain):
    widened = signal.astype(F32)
    average = jnp.mean(widened, axis=-1, keepdims=True)
    centred = widened - average
    variance = jnp.mean(centred * centred, axis=-1, keepdims=True)
    return (centred * lax.rsqrt(variance + LN_EPSILON) * gain).astype(BF)


def nn(a, b):
    return lax.dot_general(a, b, (((1,), (0,)), ((), ())), preferred_element_type=F32)


def prep_kernel(own, left, right, ids, gain, nt, audio_t, idk, idq):
    frame = lax.broadcasted_iota(jnp.int32, (256, 256), 0)
    slot = lax.broadcasted_iota(jnp.int32, (256, 256), 1)
    order = jnp.where(slot < 128, 2 * slot, 2 * slot - 255)
    place = jnp.where(frame == order, 1.0, 0.0).astype(BF)
    nt[:, 0:256] = nn(layer_norm(own[...], gain[...]).T, place).astype(BF)
    nt[:, 256:384] = layer_norm(left[:128, :], gain[...]).T
    nt[:, 384:512] = layer_norm(right[:128, :], gain[...]).T
    audio_t[...] = nn(own[...].T, place).astype(BF)
    numbers = nn(ids[...].astype(BF), place)
    idq[...] = numbers
    tags = [numbers[0:1, :], left[128:136, 0:128].astype(F32)[0:1], right[128:136, 0:128].astype(F32)[0:1]]
    idk[...] = jnp.broadcast_to(jnp.concatenate(tags, axis=1), (128, 512)).T


def load_pieces(tab, pieces, place, sems):
    copies = []
    for side in range(2):
        for p in range(4):
            for i in range(4):
                if p == 3:
                    src = pieces[side * 5 + 3 + i // 2].at[i % 2]
                else:
                    src = pieces[side * 5 + p].at[i]
                slot = p * 4 + i
                copy = pltpu.make_async_copy(
                    src, place(side, slot, tab[2 + side * 16 + slot]), sems.at[side * 16 + slot]
                )
                copy.start()
                copies.append(copy)
    return copies


def project_kernel(tab, nt, *refs):
    pieces, (qkv, w, sems) = refs[:10], refs[10:]
    core = tab[0]
    copies = load_pieces(
        tab, pieces, lambda side, slot, g: w.at[side, pl.ds(pl.multiple_of(g * 240, 16), 240), :], sems
    )
    for copy in copies:
        copy.wait()
    own = pl.ds(pl.multiple_of(core * 640, 128), 640)
    oth = pl.ds(pl.multiple_of(640 - core * 640, 128), 640)

    def query_rows(m, carry):
        rows = pl.ds(pl.multiple_of(m * 640, 128), 640)
        acc = nn(w[0, rows, :], nt[own, 0:256]) + nn(w[1, rows, :], nt[oth, 0:256])
        qkv[rows, 0:256] = acc.astype(BF) * BF(HEAD**-0.5)
        return carry

    def pair_rows(m, carry):
        rows = pl.ds(pl.multiple_of(m * 640, 128), 640)
        acc = nn(w[0, rows, :], nt[own, :]) + nn(w[1, rows, :], nt[oth, :])
        qkv[rows, :] = acc.astype(BF)
        return carry

    lax.fori_loop(0, 2, query_rows, 0)
    lax.fori_loop(2, 6, pair_rows, 0)


def heads_kernel(first, count, qkv, idk, idq, out, bias):
    bias[...] = jnp.where(idk[:, 0:1] == idq[0:1, :], 0.0, MASKED)

    def one_head(h):
        base = (first + h) * HEAD
        q = qkv[pl.ds(pl.multiple_of(base, 64), HEAD), 0:256]
        k = qkv[pl.ds(pl.multiple_of(D + base, 64), HEAD), :]
        v = qkv[pl.ds(pl.multiple_of(2 * D + base, 64), HEAD), :]
        s = nn(k.T, q) + bias[...]
        top = jnp.max(s, axis=0, keepdims=True)
        e = jnp.exp(s - top)
        total = jnp.sum(e, axis=0, keepdims=True)
        o = nn(v, e.astype(BF)) / total
        out[pl.ds(pl.multiple_of(h * HEAD, 64), HEAD), :] = o.astype(BF)

    def pair(n, carry):
        one_head(2 * n)
        one_head(2 * n + 1)
        return carry

    lax.fori_loop(0, count // 2, pair, 0)


def tail_kernel(tab, att0, att1, audio_t, gain, meta, *refs):
    pieces = refs[:10]
    thinker, x0, x1, w, wo, enc_t, acc, rider, sems = refs[10:]
    core = tab[0]
    copies = load_pieces(tab, pieces, lambda side, slot, g: w.at[side, slot], sems)
    for side in range(2):
        for s in range(16):
            copies[side * 16 + s].wait()
            row = pl.multiple_of(tab[2 + side * 16 + s] * 80, 16)
            half = core if side == 0 else 1 - core
            for k in range(5):
                wo[half, pl.ds(row, 80), k * 128 : (k + 1) * 128] = w[side, s, k * 80 : (k + 1) * 80, :]

    def project(m, carry):
        rows = pl.ds(pl.multiple_of(m * 640, 128), 640)
        projected = nn(wo[0, rows, :], att0[...]) + nn(wo[1, rows, :], att1[...])
        enc_t[rows, :] = (audio_t[rows, :].astype(F32) + projected).astype(BF)
        return carry

    lax.fori_loop(0, 2, project, 0)
    even = enc_t[:, 0:128].T
    odd = enc_t[:, 128:256].T
    first = core == 0
    mine = jnp.where(first, even, odd)
    rest = jnp.where(first, odd, even)

    def columns(n, carry):
        p, i = n // 2, n % 2
        s, t = p * 4 + 2 * i, 8 * i + p
        both = jnp.concatenate([w[0, s, 400:1680, :], w[0, s + 1, 400:1680, :]], axis=1)
        block = nn(mine, both)
        both = jnp.concatenate([w[1, t, 400:1680, :], w[1, t + 4, 400:1680, :]], axis=1)
        block = block + nn(rest, both)
        acc[:, pl.ds(pl.multiple_of(tab[2 + s] * 128, 128), 128)] = block[:, :128]
        acc[:, pl.ds(pl.multiple_of(tab[3 + s] * 128, 128), 128)] = block[:, 128:]
        return carry

    lax.fori_loop(0, 8, columns, 0)
    rounded = acc[...].astype(BF)
    thinker[...] = rounded
    widened = rounded.astype(F32)
    squares = jnp.mean(widened * widened, axis=1, keepdims=True)
    normed = (widened * lax.rsqrt(squares + RMS_EPSILON) * gain[...]).astype(BF)
    x0[0:128, :] = normed[:, :HALF]
    rider[...] = jnp.zeros((8, HALF), F32)
    for k in range(4):
        one = slice(k * 128, (k + 1) * 128)
        two = slice(512 + k * 128, 512 + (k + 1) * 128)
        share = meta[4 + k : 5 + k, :]
        high = share.astype(BF).astype(F32)
        middle = (share - high).astype(BF).astype(F32)
        rider[0:1, one] = meta[k : k + 1, :]
        rider[0:1, two] = high
        rider[1:2, one] = middle
        rider[1:2, two] = share - high - middle
    x0[128:136, :] = rider[...].astype(BF)
    x1[...] = normed[:, HALF:]


def expert_kernel(tab, *refs):
    xs, weights = refs[:16], refs[16:22]
    outs = refs[22:38]
    wg, wu, wd, xg, hid, yg, dsel, share, sems = refs[38:]
    core, z = tab[0], tab[1]
    copies = []
    for n, (src, dst) in enumerate(
        zip(weights, (wg.at[0], wu.at[0], wd.at[0], wg.at[1], wu.at[1], wd.at[1]))
    ):
        copy = pltpu.make_async_copy(src, dst, sems.at[n])
        copy.start()
        copies.append(copy)
    e0 = (2 * z + core).astype(F32)
    e1 = (2 * z + 1 - core).astype(F32)
    lane = lax.broadcasted_iota(jnp.int32, (128, 128), 1)
    sub = lax.broadcasted_iota(jnp.int32, (128, 128), 0)
    expert = jnp.where(sub < CAP, e0, e1)
    slot = jnp.where(sub < CAP, sub, sub - CAP).astype(F32)
    earlier = jnp.where(sub < lane, 1.0, 0.0).astype(BF)
    for r in range(8):
        rider = xs[2 * r][128:136, :].astype(F32)
        chosen = jnp.zeros((128, 128), F32)
        weight = jnp.zeros((128, 128), F32)
        for k in range(4):
            one = slice(k * 128, (k + 1) * 128)
            two = slice(512 + k * 128, 512 + (k + 1) * 128)
            hit = rider[0:1, one] == expert
            chosen = jnp.where(hit, 1.0, chosen)
            weight = jnp.where(hit, rider[0:1, two] + rider[1:2, one] + rider[1:2, two], weight)
        place = nn(chosen.astype(BF), earlier)
        select = jnp.where((place == slot) & (sub < 2 * CAP), chosen, 0.0)
        dsel[r] = select.T.astype(BF)
        share[r] = jnp.broadcast_to(jnp.sum(select * weight, axis=1, keepdims=True), (128, 128))
        pick = select[: 2 * CAP].astype(BF)
        for j in range(2):
            rows = nn(pick, xs[2 * r + j][0:128, :]).astype(BF)
            xg[0, r * CAP : (r + 1) * CAP, j * HALF : (j + 1) * HALF] = rows[:CAP]
            xg[1, r * CAP : (r + 1) * CAP, j * HALF : (j + 1) * HALF] = rows[CAP:]
        yg[r, 2 * CAP :, :] = jnp.zeros((128 - 2 * CAP, DM), BF)
    for e in range(2):
        copies[3 * e].wait()
        copies[3 * e + 1].wait()

        def up(n, carry):
            cols = pl.ds(pl.multiple_of(n * 256, 256), 256)
            gate_act = nn(xg[e], wg[e, :, cols])
            up_act = nn(xg[e], wu[e, :, cols])
            hid[:, cols] = (gate_act / (1.0 + jnp.exp(-gate_act)) * up_act).astype(BF)
            return carry

        lax.fori_loop(0, FF // 256, up, 0)
        copies[3 * e + 2].wait()

        def down(n, carry):
            cols = pl.ds(pl.multiple_of(n * 256, 256), 256)
            made = nn(hid[...], wd[e, :, cols])
            for r in range(8):
                scale = share[r, e * CAP : (e + 1) * CAP, 0:1]
                yg[r, e * CAP : (e + 1) * CAP, cols] = (
                    made[r * CAP : (r + 1) * CAP] * scale
                ).astype(BF)
            return carry

        lax.fori_loop(0, DM // 256, down, 0)
    for r in range(8):
        for j in range(2):
            outs[2 * r + j][...] = nn(dsel[r], yg[r, :, j * HALF : (j + 1) * HALF]).astype(BF)


VMEM = pl.BlockSpec(memory_space=pltpu.VMEM)
SMEM = pl.BlockSpec(memory_space=pltpu.SMEM)
HBM = pl.BlockSpec(memory_space=pltpu.HBM)


def shape(*dims, dtype=BF):
    return jax.ShapeDtypeStruct(dims, dtype)


def layer(
    audio,
    block_ids,
    norm_gain,
    qkv_weight,
    out_weight,
    adapter_weight,
    moe_gain,
    gate_weight,
    up_weight,
    down_weight,
    routes,
    route_weights,
):
    y, x = lax.axis_index("y"), lax.axis_index("x")
    z, core = lax.axis_index("z"), lax.axis_index("core")

    count = NZ * 2
    ahead = [(i, i + 1) for i in range(count - 1)]
    back = [(i + 1, i) for i in range(count - 1)]
    signal = audio[0]
    weights_here = route_weights[0]
    shares = weights_here / jnp.sum(weights_here, axis=1, keepdims=True)
    meta = jnp.concatenate([routes[0].astype(F32).T, shares.T])
    tags = (block_ids[0] + 1).astype(F32)
    rider = jnp.pad(tags.astype(BF).reshape(2, 1, 128), ((0, 0), (0, 7), (0, 1280 - 128)))
    to_right = jnp.concatenate([signal[128:], rider[1]])
    to_left = jnp.concatenate([signal[:128], rider[0]])
    mine = lax.dynamic_slice_in_dim(qkv_weight.T, core * 640, 640, 1)
    out_t = lax.dynamic_slice_in_dim(out_weight.T, core * 640, 640, 1)
    out_t = out_t.reshape(80, 5, 128).transpose(1, 0, 2).reshape(400, 128)
    ada = lax.dynamic_slice_in_dim(adapter_weight, core * D, D, 0)
    oa_mine = jnp.concatenate([out_t, ada])
    near = ring_step(mine, mine, 0)
    oa_near = ring_step(oa_mine, oa_mine, 0)
    a, b, oa_a, oa_b, to_right, to_left = join(*near, *oa_near, to_right, to_left)
    near = ring_step(a[:128], b[128:], 0)
    oa_near = ring_step(oa_a[:848], oa_b[848:], 0)
    o0, o1, oa_o0, oa_o1, left, right = join(
        *near,
        *oa_near,
        lax.ppermute(to_right, SEQ, ahead),
        lax.ppermute(to_left, SEQ, back),
    )
    block = jnp.stack([mine, a, b, jnp.concatenate([o0, o1])])
    oa_block = jnp.stack([oa_mine, oa_a, oa_b, jnp.concatenate([oa_o0, oa_o1])])

    normed_t, audio_t, idk, idq = pl.pallas_call(
        prep_kernel,
        out_shape=[
            shape(D, 512),
            shape(D, 256),
            shape(512, 128, dtype=F32),
            shape(8, 256, dtype=F32),
        ],
        in_specs=[VMEM] * 5,
        out_specs=[VMEM] * 4,
        cost_estimate=pl.CostEstimate(flops=10**9, bytes_accessed=4 * 10**6, transcendentals=0),
        name="prep",
    )(signal, left, right, jnp.broadcast_to(tags[None], (8, 256)), norm_gain[None])

    ring = ring_step(block, block, 1)
    s_own = swap_cores(block)
    qa, qb, s_own, normed_t, audio_t, idk, idq, meta, oa_block = join(
        *ring, s_own, normed_t, audio_t, idk, idq, meta, oa_block
    )
    far = ring_step(qa[:2], qb[2:], 1)
    swaps = swap_cores(qa), swap_cores(qb)
    qo0, qo1, s_a, s_b, oa_block = join(*far, *swaps, oa_block)
    qkv_own = (block, qa, qb, qo0, qo1)
    oa_a, oa_b = ring_step(oa_block, oa_block, 1)
    s_o0, s_o1 = join(swap_cores(qo0), swap_cores(qo1))
    qkv_other = (s_own, s_a, s_b, s_o0, s_o1)
    oa_s = swap_cores(oa_block)
    gate_other = swap_cores(join(gate_weight[0], s_o0, s_o1)[0])

    rel = jnp.array(REL, jnp.int32)
    at_y, at_x = (y + rel) % NY, (x + rel) % NX
    table0 = at_y[:, None] * NX + at_x[None, :]
    table1 = at_y[None, :] * NX + at_x[:, None]
    own_table = jnp.where(core == 0, table0, table1).reshape(-1)
    other_table = jnp.where(core == 0, table1, table0).reshape(-1)
    tab = jnp.concatenate([jnp.stack([core, z]), own_table, other_table]).astype(jnp.int32)

    qkv = pl.pallas_call(
        project_kernel,
        out_shape=shape(3 * D, 512),
        in_specs=[SMEM, VMEM] + [HBM] * 10,
        out_specs=VMEM,
        scratch_shapes=[pltpu.VMEM((2, 3 * D, 640), BF), pltpu.SemaphoreType.DMA((32,))],
        compiler_params=pltpu.CompilerParams(vmem_limit_bytes=57 << 20),
        cost_estimate=pl.CostEstimate(flops=5 * 10**9, bytes_accessed=15 * 10**6, transcendentals=0),
        name="project",
    )(tab, normed_t, *qkv_own, *qkv_other)

    def attend(qkv, first_head):
        return pl.pallas_call(
            functools.partial(heads_kernel, first_head, HEADS // 2),
            out_shape=shape(D // 2, 256),
            in_specs=[VMEM] * 3,
            out_specs=VMEM,
            scratch_shapes=[pltpu.VMEM((512, 256), F32)],
            compiler_params=pltpu.CompilerParams(vmem_limit_bytes=56 << 20),
                cost_estimate=pl.CostEstimate(
                flops=5 * 10**9, bytes_accessed=4 * 10**6, transcendentals=10**6
            ),
            name="heads",
        )(qkv, idk, idq)

    up_other = swap_cores(join(up_weight[0], qkv)[0])
    attended0 = attend(qkv, 0)
    attended0, qkv, oa_a, oa_b, oa_s = join(attended0, qkv, oa_a, oa_b, oa_s)
    far = ring_step(oa_a[:2], oa_b[2:], 1)
    swaps = swap_cores(oa_a), swap_cores(oa_b)
    attended1, oa_o0, oa_o1, oa_sa, oa_sb = join(attend(qkv, HEADS // 2), *far, *swaps)
    oa_so0, oa_so1 = join(swap_cores(oa_o0), swap_cores(oa_o1))
    attended = (attended0, attended1)
    oa_own = (oa_block, oa_a, oa_b, oa_o0, oa_o1)
    oa_other = (oa_s, oa_sa, oa_sb, oa_so0, oa_so1)
    down_other = swap_cores(join(down_weight[0], oa_so1)[0])
    expert_other = (gate_other, up_other, down_other)

    thinker_in, x0, x1 = pl.pallas_call(
        tail_kernel,
        out_shape=[shape(128, DM), shape(136, HALF), shape(128, HALF)],
        in_specs=[SMEM, VMEM, VMEM, VMEM, VMEM, VMEM] + [HBM] * 10,
        out_specs=[VMEM] * 3,
        scratch_shapes=[
            pltpu.VMEM((2, 16, 1680, 128), BF),
            pltpu.VMEM((2, D, 640), BF),
            pltpu.VMEM((D, 256), BF),
            pltpu.VMEM((128, DM), F32),
            pltpu.VMEM((8, HALF), F32),
            pltpu.SemaphoreType.DMA((32,)),
        ],
        cost_estimate=pl.CostEstimate(flops=3 * 10**9, bytes_accessed=16 * 10**6, transcendentals=0),
        name="tail",
    )(tab, *attended, audio_t, moe_gain[None], meta, *oa_own, *oa_other)

    up0, up1, down0, down1 = [x0], [x1], [x0], [x1]
    for step in range(4):
        up0.append(shift_z(up0[-1], 1))
        down1.append(shift_z(down1[-1], -1))
        if step < 3:
            up1.append(shift_z(up1[-1], 1))
            down0.append(shift_z(down0[-1], -1))

    def tokens_from(off):
        if off == 4:
            return [up0[4], down1[4]]
        return [up0[-off], up1[-off]] if off <= 0 else [down0[off], down1[off]]

    partial = pl.pallas_call(
        expert_kernel,
        out_shape=[shape(128, HALF)] * 16,
        in_specs=[SMEM] + [VMEM] * 16 + [HBM] * 6,
        out_specs=[VMEM] * 16,
        scratch_shapes=[
            pltpu.VMEM((2, DM, FF), BF),
            pltpu.VMEM((2, DM, FF), BF),
            pltpu.VMEM((2, FF, DM), BF),
            pltpu.VMEM((2, 8 * CAP, DM), BF),
            pltpu.VMEM((8 * CAP, FF), BF),
            pltpu.VMEM((8, 128, DM), BF),
            pltpu.VMEM((8, 128, 128), BF),
            pltpu.VMEM((8, 128, 128), F32),
            pltpu.SemaphoreType.DMA((6,)),
        ],
        cost_estimate=pl.CostEstimate(
            flops=8 * 10**9, bytes_accessed=28 * 10**6, transcendentals=10**6
        ),
        name="experts",
    )(
        tab,
        *[v for off in ZREL for v in tokens_from(off)],
        gate_weight[0],
        up_weight[0],
        down_weight[0],
        *expert_other,
    )
    by_off = {off: partial[2 * n : 2 * n + 2] for n, off in enumerate(ZREL)}

    def add(a, b):
        return (a.astype(F32) + b.astype(F32)).astype(BF)

    def back_along(j, sign, far):
        total = by_off[far if far == 4 else sign * far][j]
        for off in range(far - 1, 0, -1):
            total = add(shift_z(total, sign), by_off[sign * off][j])
        return shift_z(total, sign)

    halves = []
    for j in range(2):
        from_left = back_along(j, 1, 4 if j == 0 else 3)
        from_right = back_along(j, -1, 3 if j == 0 else 4)
        base = thinker_in[:, j * HALF : (j + 1) * HALF].astype(F32)
        total = base + by_off[0][j].astype(F32) + from_left.astype(F32) + from_right.astype(F32)
        halves.append(total.astype(BF))
    return jnp.concatenate(halves, axis=1)[None]


def solution(mesh):
    torus = Mesh(mesh.devices.reshape(NY, NX, NZ, 2), ALL)
    in_specs = (
        P(GRP, SEQ, None),
        P(GRP, SEQ),
        P(),
        P(None, GRP),
        P(None, GRP),
        P(None, GRP),
        P(),
        P(SEQ, None, None),
        P(SEQ, None, None),
        P(SEQ, None, None),
        P(GRP, SEQ, None),
        P(GRP, SEQ, None),
    )
    out_specs = P(GRP, SEQ, None)
    return jax.shard_map(layer, mesh=torus, in_specs=in_specs, out_specs=out_specs, check_vma=False)
```

```python
import functools

import jax
import jax.numpy as jnp
from jax import lax
from jax.experimental import pallas as pl
from jax.experimental.pallas import tpu as pltpu
from jax.sharding import Mesh
from jax.sharding import PartitionSpec as P


HEADS = 20
HEAD = 64
D = 1280
DM = 2048
FF = 768
CAP = 48
GRP = ("y", "x")
SEQ = ("z", "core")
ALL = ("y", "x", "z", "core")
NY, NX, NZ = 4, 4, 8
LN_EPSILON = 1e-05
RMS_EPSILON = 1e-06
MASKED = -1e30
BF = jnp.bfloat16
F32 = jnp.float32

REL = (0, -1, 1, 2)
ZREL = (0, -1, 1, -2, 2, -3, 3, 4)
HALF = DM // 2


def flat(y, x, z, c):
    return (((y % NY) * NX + x % NX) * NZ + z % NZ) * 2 + c


def grp_perm(phase, sign):
    pairs = []
    for y in range(NY):
        for x in range(NX):
            for z in range(NZ):
                for c in range(2):
                    along_x = (c == 0) == (phase == 0)
                    dst = flat(y, x + sign, z, c) if along_x else flat(y + sign, x, z, c)
                    pairs.append((flat(y, x, z, c), dst))
    return pairs


def swap_cores(value):
    return lax.ppermute(value, "core", [(0, 1), (1, 0)])


def shift_z(value, sign):
    return lax.ppermute(value, "z", [(i, (i + sign) % NZ) for i in range(NZ)])


def join(*values):
    return lax.optimization_barrier(values)


def ring_step(first, second, phase):
    move = functools.partial(lax.ppermute, axis_name=ALL)
    return move(first, perm=grp_perm(phase, 1)), move(second, perm=grp_perm(phase, -1))


def layer_norm(signal, gain):
    widened = signal.astype(F32)
    average = jnp.mean(widened, axis=-1, keepdims=True)
    centred = widened - average
    variance = jnp.mean(centred * centred, axis=-1, keepdims=True)
    return (centred * lax.rsqrt(variance + LN_EPSILON) * gain).astype(BF)


def nn(a, b):
    return lax.dot_general(a, b, (((1,), (0,)), ((), ())), preferred_element_type=F32)


def prep_kernel(own, left, right, ids, gain, nt, audio_t, idk, idq):
    frame = lax.broadcasted_iota(jnp.int32, (256, 256), 0)
    slot = lax.broadcasted_iota(jnp.int32, (256, 256), 1)
    order = jnp.where(slot < 128, 2 * slot, 2 * slot - 255)
    place = jnp.where(frame == order, 1.0, 0.0).astype(BF)
    nt[:, 0:256] = nn(layer_norm(own[...], gain[...]).T, place).astype(BF)
    nt[:, 256:384] = layer_norm(left[:128, :], gain[...]).T
    nt[:, 384:512] = layer_norm(right[:128, :], gain[...]).T
    audio_t[...] = nn(own[...].T, place).astype(BF)
    numbers = nn(ids[...].astype(BF), place)
    idq[...] = numbers
    tags = [numbers[0:1, :], left[128:136, 0:128].astype(F32)[0:1], right[128:136, 0:128].astype(F32)[0:1]]
    idk[...] = jnp.broadcast_to(jnp.concatenate(tags, axis=1), (128, 512)).T


def load_pieces(tab, pieces, place, sems):
    copies = []
    for side in range(2):
        for p in range(4):
            for i in range(4):
                if p == 3:
                    src = pieces[side * 5 + 3 + i // 2].at[i % 2]
                else:
                    src = pieces[side * 5 + p].at[i]
                slot = p * 4 + i
                copy = pltpu.make_async_copy(
                    src, place(side, slot, tab[2 + side * 16 + slot]), sems.at[side * 16 + slot]
                )
                copy.start()
                copies.append(copy)
    return copies


def project_kernel(tab, nt, *refs):
    pieces, (qkv, w, sems) = refs[:10], refs[10:]
    core = tab[0]
    copies = load_pieces(
        tab, pieces, lambda side, slot, g: w.at[side, pl.ds(pl.multiple_of(g * 240, 16), 240), :], sems
    )
    for copy in copies:
        copy.wait()
    own = pl.ds(pl.multiple_of(core * 640, 128), 640)
    oth = pl.ds(pl.multiple_of(640 - core * 640, 128), 640)

    def query_rows(m, carry):
        rows = pl.ds(pl.multiple_of(m * 640, 128), 640)
        acc = nn(w[0, rows, :], nt[own, 0:256]) + nn(w[1, rows, :], nt[oth, 0:256])
        qkv[rows, 0:256] = acc.astype(BF) * BF(HEAD**-0.5)
        return carry

    def pair_rows(m, carry):
        rows = pl.ds(pl.multiple_of(m * 640, 128), 640)
        acc = nn(w[0, rows, :], nt[own, :]) + nn(w[1, rows, :], nt[oth, :])
        qkv[rows, :] = acc.astype(BF)
        return carry

    lax.fori_loop(0, 2, query_rows, 0)
    lax.fori_loop(2, 6, pair_rows, 0)


def heads_kernel(first, count, qkv, idk, idq, out, bias):
    bias[...] = jnp.where(idk[:, 0:1] == idq[0:1, :], 0.0, MASKED)

    def one_head(h):
        base = (first + h) * HEAD
        q = qkv[pl.ds(pl.multiple_of(base, 64), HEAD), 0:256]
        k = qkv[pl.ds(pl.multiple_of(D + base, 64), HEAD), :]
        v = qkv[pl.ds(pl.multiple_of(2 * D + base, 64), HEAD), :]
        s = nn(k.T, q) + bias[...]
        top = jnp.max(s, axis=0, keepdims=True)
        e = jnp.exp(s - top)
        total = jnp.sum(e, axis=0, keepdims=True)
        o = nn(v, e.astype(BF)) / total
        out[pl.ds(pl.multiple_of(h * HEAD, 64), HEAD), :] = o.astype(BF)

    def pair(n, carry):
        one_head(2 * n)
        one_head(2 * n + 1)
        return carry

    lax.fori_loop(0, count // 2, pair, 0)


def tail_kernel(tab, att0, att1, audio_t, gain, meta, *refs):
    pieces = refs[:10]
    thinker, x0, x1, w, wo, enc_t, acc, rider, sems = refs[10:]
    core = tab[0]
    copies = load_pieces(tab, pieces, lambda side, slot, g: w.at[side, slot], sems)
    for side in range(2):
        for s in range(16):
            copies[side * 16 + s].wait()
            row = pl.multiple_of(tab[2 + side * 16 + s] * 80, 16)
            half = core if side == 0 else 1 - core
            for k in range(5):
                wo[half, pl.ds(row, 80), k * 128 : (k + 1) * 128] = w[side, s, k * 80 : (k + 1) * 80, :]

    def project(m, carry):
        rows = pl.ds(pl.multiple_of(m * 640, 128), 640)
        projected = nn(wo[0, rows, :], att0[...]) + nn(wo[1, rows, :], att1[...])
        enc_t[rows, :] = (audio_t[rows, :].astype(F32) + projected).astype(BF)
        return carry

    lax.fori_loop(0, 2, project, 0)
    even = enc_t[:, 0:128].T
    odd = enc_t[:, 128:256].T
    first = core == 0
    mine = jnp.where(first, even, odd)
    rest = jnp.where(first, odd, even)

    def columns(n, carry):
        p, i = n // 2, n % 2
        s, t = p * 4 + 2 * i, 8 * i + p
        both = jnp.concatenate([w[0, s, 400:1680, :], w[0, s + 1, 400:1680, :]], axis=1)
        block = nn(mine, both)
        both = jnp.concatenate([w[1, t, 400:1680, :], w[1, t + 4, 400:1680, :]], axis=1)
        block = block + nn(rest, both)
        acc[:, pl.ds(pl.multiple_of(tab[2 + s] * 128, 128), 128)] = block[:, :128]
        acc[:, pl.ds(pl.multiple_of(tab[3 + s] * 128, 128), 128)] = block[:, 128:]
        return carry

    lax.fori_loop(0, 8, columns, 0)
    rounded = acc[...].astype(BF)
    thinker[...] = rounded
    widened = rounded.astype(F32)
    squares = jnp.mean(widened * widened, axis=1, keepdims=True)
    normed = (widened * lax.rsqrt(squares + RMS_EPSILON) * gain[...]).astype(BF)
    x0[0:128, :] = normed[:, :HALF]
    rider[...] = jnp.zeros((8, HALF), F32)
    for k in range(4):
        one = slice(k * 128, (k + 1) * 128)
        two = slice(512 + k * 128, 512 + (k + 1) * 128)
        share = meta[4 + k : 5 + k, :]
        high = share.astype(BF).astype(F32)
        middle = (share - high).astype(BF).astype(F32)
        rider[0:1, one] = meta[k : k + 1, :]
        rider[0:1, two] = high
        rider[1:2, one] = middle
        rider[1:2, two] = share - high - middle
    x0[128:136, :] = rider[...].astype(BF)
    x1[...] = normed[:, HALF:]


def expert_kernel(tab, *refs):
    xs, (gate, up_w, down_w, pair, down_o) = refs[:16], refs[16:21]
    outs = refs[21:37]
    wg, wu, wd, xg, hid, yg, dsel, share, sems = refs[37:]
    weights = (gate, up_w, down_w, pair.at[0:DM], pair.at[DM : 2 * DM], down_o)
    core, z = tab[0], tab[1]
    copies = []
    for n, (src, dst) in enumerate(
        zip(weights, (wg.at[0], wu.at[0], wd.at[0], wg.at[1], wu.at[1], wd.at[1]))
    ):
        copy = pltpu.make_async_copy(src, dst, sems.at[n])
        copy.start()
        copies.append(copy)
    e0 = (2 * z + core).astype(F32)
    e1 = (2 * z + 1 - core).astype(F32)
    lane = lax.broadcasted_iota(jnp.int32, (128, 128), 1)
    sub = lax.broadcasted_iota(jnp.int32, (128, 128), 0)
    expert = jnp.where(sub < CAP, e0, e1)
    slot = jnp.where(sub < CAP, sub, sub - CAP).astype(F32)
    earlier = jnp.where(sub < lane, 1.0, 0.0).astype(BF)
    for r in range(8):
        rider = xs[2 * r][128:136, :].astype(F32)
        chosen = jnp.zeros((128, 128), F32)
        weight = jnp.zeros((128, 128), F32)
        for k in range(4):
            one = slice(k * 128, (k + 1) * 128)
            two = slice(512 + k * 128, 512 + (k + 1) * 128)
            hit = rider[0:1, one] == expert
            chosen = jnp.where(hit, 1.0, chosen)
            weight = jnp.where(hit, rider[0:1, two] + rider[1:2, one] + rider[1:2, two], weight)
        place = nn(chosen.astype(BF), earlier)
        select = jnp.where((place == slot) & (sub < 2 * CAP), chosen, 0.0)
        dsel[r] = select.T.astype(BF)
        share[r] = jnp.broadcast_to(jnp.sum(select * weight, axis=1, keepdims=True), (128, 128))
        pick = select[: 2 * CAP].astype(BF)
        for j in range(2):
            rows = nn(pick, xs[2 * r + j][0:128, :]).astype(BF)
            xg[0, r * CAP : (r + 1) * CAP, j * HALF : (j + 1) * HALF] = rows[:CAP]
            xg[1, r * CAP : (r + 1) * CAP, j * HALF : (j + 1) * HALF] = rows[CAP:]
        yg[r, 2 * CAP :, :] = jnp.zeros((128 - 2 * CAP, DM), BF)
    for e in range(2):
        copies[3 * e].wait()
        copies[3 * e + 1].wait()

        def up(n, carry):
            cols = pl.ds(pl.multiple_of(n * 256, 256), 256)
            gate_act = nn(xg[e], wg[e, :, cols])
            up_act = nn(xg[e], wu[e, :, cols])
            hid[:, cols] = (gate_act / (1.0 + jnp.exp(-gate_act)) * up_act).astype(BF)
            return carry

        lax.fori_loop(0, FF // 256, up, 0)
        copies[3 * e + 2].wait()

        def down(n, carry):
            cols = pl.ds(pl.multiple_of(n * 256, 256), 256)
            made = nn(hid[...], wd[e, :, cols])
            for r in range(8):
                scale = share[r, e * CAP : (e + 1) * CAP, 0:1]
                yg[r, e * CAP : (e + 1) * CAP, cols] = (
                    made[r * CAP : (r + 1) * CAP] * scale
                ).astype(BF)
            return carry

        lax.fori_loop(0, DM // 256, down, 0)
    for r in range(8):
        for j in range(2):
            outs[2 * r + j][...] = nn(dsel[r], yg[r, :, j * HALF : (j + 1) * HALF]).astype(BF)


VMEM = pl.BlockSpec(memory_space=pltpu.VMEM)
SMEM = pl.BlockSpec(memory_space=pltpu.SMEM)
ANY = pl.BlockSpec(memory_space=pl.ANY)


def shape(*dims, dtype=BF):
    return jax.ShapeDtypeStruct(dims, dtype)


def layer(
    audio,
    block_ids,
    norm_gain,
    qkv_weight,
    out_weight,
    adapter_weight,
    moe_gain,
    gate_weight,
    up_weight,
    down_weight,
    routes,
    route_weights,
):
    y, x = lax.axis_index("y"), lax.axis_index("x")
    z, core = lax.axis_index("z"), lax.axis_index("core")

    count = NZ * 2
    ahead = [(i, i + 1) for i in range(count - 1)]
    back = [(i + 1, i) for i in range(count - 1)]
    signal = audio[0]
    weights_here = route_weights[0]
    shares = weights_here / jnp.sum(weights_here, axis=1, keepdims=True)
    meta = jnp.concatenate([routes[0].astype(F32).T, shares.T])
    tags = (block_ids[0] + 1).astype(F32)
    rider = jnp.pad(tags.astype(BF).reshape(2, 1, 128), ((0, 0), (0, 7), (0, 1280 - 128)))
    to_right = jnp.concatenate([signal[128:], rider[1]])
    to_left = jnp.concatenate([signal[:128], rider[0]])
    mine = lax.dynamic_slice_in_dim(qkv_weight.T, core * 640, 640, 1)
    a, b = join(*ring_step(mine, mine, 0))
    o0, o1, left, right = join(
        *ring_step(a[:128], b[128:], 0),
        lax.ppermute(to_right, SEQ, ahead),
        lax.ppermute(to_left, SEQ, back),
    )
    block = jnp.stack([mine, a, b, jnp.concatenate([o0, o1])])

    normed_t, audio_t, idk, idq = pl.pallas_call(
        prep_kernel,
        out_shape=[
            shape(D, 512),
            shape(D, 256),
            shape(512, 128, dtype=F32),
            shape(8, 256, dtype=F32),
        ],
        in_specs=[VMEM] * 5,
        out_specs=[VMEM] * 4,
        cost_estimate=pl.CostEstimate(flops=10**9, bytes_accessed=4 * 10**6, transcendentals=0),
        name="prep",
    )(signal, left, right, jnp.broadcast_to(tags[None], (8, 256)), norm_gain[None])

    out_t = lax.dynamic_slice_in_dim(out_weight.T, core * 640, 640, 1)
    out_t = out_t.reshape(80, 5, 128).transpose(1, 0, 2).reshape(400, 128)
    ada = lax.dynamic_slice_in_dim(adapter_weight, core * D, D, 0)
    oa_mine = jnp.concatenate([out_t, ada])
    oa_mine = join(oa_mine, o0)[0]
    pair = jnp.concatenate([gate_weight[0], join(up_weight[0], o0)[0]])
    qa, qb, a, b, s_own, normed_t, audio_t, idk, idq, meta, pair = join(
        *ring_step(block, block, 1),
        *ring_step(oa_mine, oa_mine, 0),
        swap_cores(block),
        normed_t,
        audio_t,
        idk,
        idq,
        meta,
        pair,
    )
    far = ring_step(qa[:2], qb[2:], 1)
    swaps = swap_cores(qa), swap_cores(qb)
    qo0, qo1, o0, o1, s_a, s_b = join(*far, *ring_step(a[:848], b[848:], 0), *swaps)
    oa_block = jnp.stack([oa_mine, a, b, jnp.concatenate([o0, o1])])
    qkv_own = (block, qa, qb, qo0, qo1)
    s_o0, s_o1 = swap_cores(qo0), swap_cores(qo1)
    qkv_other = (s_own, s_a, s_b, s_o0, s_o1)
    oa_a, oa_b = ring_step(oa_block, oa_block, 1)
    oa_s = swap_cores(oa_block)
    down_other = swap_cores(join(down_weight[0], s_o0, s_o1)[0])

    rel = jnp.array(REL, jnp.int32)
    at_y, at_x = (y + rel) % NY, (x + rel) % NX
    table0 = at_y[:, None] * NX + at_x[None, :]
    table1 = at_y[None, :] * NX + at_x[:, None]
    own_table = jnp.where(core == 0, table0, table1).reshape(-1)
    other_table = jnp.where(core == 0, table1, table0).reshape(-1)
    tab = jnp.concatenate([jnp.stack([core, z]), own_table, other_table]).astype(jnp.int32)

    qkv = pl.pallas_call(
        project_kernel,
        out_shape=shape(3 * D, 512),
        in_specs=[SMEM, VMEM] + [ANY] * 10,
        out_specs=VMEM,
        scratch_shapes=[pltpu.VMEM((2, 3 * D, 640), BF), pltpu.SemaphoreType.DMA((32,))],
        compiler_params=pltpu.CompilerParams(vmem_limit_bytes=24 << 20),
        cost_estimate=pl.CostEstimate(flops=5 * 10**9, bytes_accessed=15 * 10**6, transcendentals=0),
        name="project",
    )(tab, normed_t, *qkv_own, *qkv_other)

    def attend(qkv, first_head):
        return pl.pallas_call(
            functools.partial(heads_kernel, first_head, HEADS // 2),
            out_shape=shape(D // 2, 256),
            in_specs=[VMEM] * 3,
            out_specs=VMEM,
            scratch_shapes=[pltpu.VMEM((512, 256), F32)],
            compiler_params=pltpu.CompilerParams(vmem_limit_bytes=12 << 20),
                cost_estimate=pl.CostEstimate(
                flops=5 * 10**9, bytes_accessed=4 * 10**6, transcendentals=10**6
            ),
            name="heads",
        )(qkv, idk, idq)

    attended0 = attend(qkv, 0)
    attended0, qkv, oa_a, oa_b, oa_s = join(attended0, qkv, oa_a, oa_b, oa_s)
    far = ring_step(oa_a[:2], oa_b[2:], 1)
    swaps = swap_cores(oa_a), swap_cores(oa_b)
    attended1, oa_o0, oa_o1, oa_sa, oa_sb = join(attend(qkv, HEADS // 2), *far, *swaps)
    oa_so0, oa_so1 = join(swap_cores(oa_o0), swap_cores(oa_o1))
    attended = (attended0, attended1)
    oa_own = (oa_block, oa_a, oa_b, oa_o0, oa_o1)
    oa_other = (oa_s, oa_sa, oa_sb, oa_so0, oa_so1)
    pair_other = swap_cores(join(pair, oa_so1)[0])

    thinker_in, x0, x1 = pl.pallas_call(
        tail_kernel,
        out_shape=[shape(128, DM), shape(136, HALF), shape(128, HALF)],
        in_specs=[SMEM, VMEM, VMEM, VMEM, VMEM, VMEM] + [ANY] * 10,
        out_specs=[VMEM] * 3,
        scratch_shapes=[
            pltpu.VMEM((2, 16, 1680, 128), BF),
            pltpu.VMEM((2, D, 640), BF),
            pltpu.VMEM((D, 256), BF),
            pltpu.VMEM((128, DM), F32),
            pltpu.VMEM((8, HALF), F32),
            pltpu.SemaphoreType.DMA((32,)),
        ],
        cost_estimate=pl.CostEstimate(flops=3 * 10**9, bytes_accessed=16 * 10**6, transcendentals=0),
        name="tail",
    )(tab, *attended, audio_t, moe_gain[None], meta, *oa_own, *oa_other)

    up0, up1, down0, down1 = [x0], [x1], [x0], [x1]
    for step in range(4):
        up0.append(shift_z(up0[-1], 1))
        down1.append(shift_z(down1[-1], -1))
        if step < 3:
            up1.append(shift_z(up1[-1], 1))
            down0.append(shift_z(down0[-1], -1))

    def tokens_from(off):
        if off == 4:
            return [up0[4], down1[4]]
        return [up0[-off], up1[-off]] if off <= 0 else [down0[off], down1[off]]

    partial = pl.pallas_call(
        expert_kernel,
        out_shape=[shape(128, HALF)] * 16,
        in_specs=[SMEM] + [VMEM] * 16 + [ANY] * 5,
        out_specs=[VMEM] * 16,
        scratch_shapes=[
            pltpu.VMEM((2, DM, FF), BF),
            pltpu.VMEM((2, DM, FF), BF),
            pltpu.VMEM((2, FF, DM), BF),
            pltpu.VMEM((2, 8 * CAP, DM), BF),
            pltpu.VMEM((8 * CAP, FF), BF),
            pltpu.VMEM((8, 128, DM), BF),
            pltpu.VMEM((8, 128, 128), BF),
            pltpu.VMEM((8, 128, 128), F32),
            pltpu.SemaphoreType.DMA((6,)),
        ],
        cost_estimate=pl.CostEstimate(
            flops=8 * 10**9, bytes_accessed=28 * 10**6, transcendentals=10**6
        ),
        name="experts",
    )(
        tab,
        *[v for off in ZREL for v in tokens_from(off)],
        gate_weight[0],
        up_weight[0],
        down_weight[0],
        pair_other,
        down_other,
    )
    by_off = {off: partial[2 * n : 2 * n + 2] for n, off in enumerate(ZREL)}

    def add(a, b):
        return (a.astype(F32) + b.astype(F32)).astype(BF)

    def back_along(j, sign, far):
        total = by_off[far if far == 4 else sign * far][j]
        for off in range(far, 0, -1):
            total = shift_z(total, sign)
            if off > 1:
                total = add(total, by_off[sign * (off - 1)][j])
        return total

    halves = []
    for j in range(2):
        from_left = back_along(j, 1, 4 if j == 0 else 3)
        from_right = back_along(j, -1, 3 if j == 0 else 4)
        base = thinker_in[:, j * HALF : (j + 1) * HALF].astype(F32)
        total = base + by_off[0][j].astype(F32) + from_left.astype(F32) + from_right.astype(F32)
        halves.append(total.astype(BF))
    return jnp.concatenate(halves, axis=1)[None]


def solution(mesh):
    torus = Mesh(mesh.devices.reshape(NY, NX, NZ, 2), ALL)
    in_specs = (
        P(GRP, SEQ, None),
        P(GRP, SEQ),
        P(),
        P(None, GRP),
        P(None, GRP),
        P(None, GRP),
        P(),
        P(SEQ, None, None),
        P(SEQ, None, None),
        P(SEQ, None, None),
        P(GRP, SEQ, None),
        P(GRP, SEQ, None),
    )
    out_specs = P(GRP, SEQ, None)
    return jax.shard_map(layer, mesh=torus, in_specs=in_specs, out_specs=out_specs, check_vma=False)
```
